32 devices in a mesh: seq: 4 (over y, core), head: 8 (over z, x).
Axes of the slice: x: 2, y: 2, z: 4, core: 2. Of those that a mesh axis runs over, the one named last changes fastest.
Arguments:
- tokens: bfloat16 [4096, 6144], P('seq', 'head'), may hold values from -6 to 6
- proj_weight: bfloat16 [4, 6144, 1024], P(None, None, 'head'), may hold values from -0.078125 to 0.078125
- decay_rate: float32 [1024], P('head'), may hold values from 5e-05 to 0.04
- norm_gain: float32 [1024], P('head'), may hold values from 0.5 to 1.5
- pool_down: bfloat16 [16, 6144, 64], P('head'), may hold values from -0.078125 to 0.078125
- pool_up: bfloat16 [16, 64, 1024], P('head'), may hold values from -0.75 to 0.75
- span_id: int32 [4, 2], replicated, may hold values from 0 to 7, as said below
- prompt_adapter: int32 [8], replicated, may hold values from 0 to 15
- owner_pos: int32 [16], replicated, may hold values from 0 to 15, each once
- slice_len: int32 [4, 2], replicated, may hold values from 1 to 512, as said below
Outputs:
- mixed_out: bfloat16 [4096, 1024], P('seq', 'head')
- end_states: float32 [4, 2, 1024, 128], P('seq', None, 'head')
The draws below stay inside these ranges and needn't reach their ends.
Inputs may be any that keep to these rules, and one draw needn't show every extreme that they name: `span_id`: along each lane, the slices of one prompt stand on consecutive seq indices and share an id; a prompt holds 1 to 4 slices; ids of different lanes differ. `slice_len`: A slice followed in its lane by a slice of the same prompt holds 512 tokens. `owner_pos`: each pool position holds exactly one adapter.
All inputs are finite; a program needn't handle non-finite values.
Results may differ from the reference program's by a relative error of at most 0.002.
The reference program's roundings to bfloat16 on the way (of `low`) count: a program that leaves them out, or rounds other values in their place, can miss the bound.
Values may be sent and summed in bfloat16 or wider, within the bound.
A program may use at most 128 MiB of HBM per device.

```python
import math
import jax
import jax.numpy as jnp
from jax import lax

D = 6144
P_SIZE = 128
R = 64
SLICE = 512
MOST = 4
LANES = 2
HEADS = 8
ADAPTERS = 16
PROMPTS = 8
TOKENS = 4096
N_SEQ = 4


def span_layout(key):
    seg_key = jax.random.fold_in(key, 7)
    seg_sizes = jax.random.randint(seg_key, (LANES, N_SEQ), 1, MOST + 1)
    seg_sizes = seg_sizes.at[0, 0].set(min(MOST, N_SEQ))
    bounds = jnp.cumsum(seg_sizes, axis=1)
    worker_index_list = jnp.arange(N_SEQ, dtype=jnp.int32)
    tallied_total = jnp.sum((bounds[:, :, None] <= worker_index_list[None, None, :]).astype(jnp.int32), axis=1)
    lane_ids = jnp.arange(LANES, dtype=jnp.int32)
    spans = (N_SEQ * LANES - 1 - (lane_ids[:, None] * N_SEQ + tallied_total)).astype(jnp.int32)
    return spans.T


def draw_span_id(key, part):
    return span_layout(key)


def draw_slice_len(key, part):
    spans = span_layout(key)
    following = jnp.concatenate([spans[1:], jnp.full((1, LANES), -1, jnp.int32)], axis=0)
    is_last = following != spans
    ragged = jax.random.randint(jax.random.fold_in(key, 11), (N_SEQ, LANES), 1, SLICE + 1)
    return jnp.where(is_last, ragged, SLICE).astype(jnp.int32)


def draw_decay_rate(key, part):
    uniform_part = jax.random.uniform(key, (HEADS * P_SIZE,), jnp.float32)
    lower, upper = (math.log(5e-05), math.log(0.04))
    return jnp.exp(lower + uniform_part * (upper - lower)).astype(jnp.float32)


def touch_ends(array, own_key, least, high):
    longest = array.shape.index(max(array.shape))
    spots = []
    for shift in (0, 1):
        where = [jax.random.randint(jax.random.fold_in(own_key, axis), (), 0, length) for axis, length in enumerate(array.shape)]
        where[longest] = (where[longest] + shift) % array.shape[longest]
        spots.append(tuple(where))
    return array.at[spots[0]].set(least).at[spots[1]].set(high)


def levels(rng, dims, pieces, low, high):
    factor_of, own = 1.0, jax.random.fold_in(rng, 6)
    for axis_at, parts in pieces:
        steps = jnp.exp(jax.random.uniform(jax.random.fold_in(own, axis_at), (parts,), jnp.float32, low / len(pieces), high / len(pieces)))
        factor_of = factor_of * jnp.repeat(steps, dims[axis_at] // parts).reshape([-1 if axis == axis_at else 1 for axis in range(len(dims))])
    return factor_of


def noise(stream_key, extent, scale, reach, pieces=(), kind=jnp.bfloat16):
    array = scale * jax.random.normal(stream_key, extent, jnp.float32)
    if pieces:
        array = array * levels(stream_key, extent, pieces, -0.22, 0.18)
    return jnp.clip(array, -reach, reach).astype(kind)


def setup_inputs(seed: int = 0) -> dict:
    streams_of = jax.random.split(jax.random.key(seed), 11)
    tokens = noise(streams_of[0], (TOKENS, D), 1.0, 6.0, ((0, 4), (1, 8)))
    proj_weight = noise(streams_of[1], (4, D, HEADS * P_SIZE), D ** -0.5, 0.078125, ((2, 8),))
    decay_rate = draw_decay_rate(jax.random.fold_in(streams_of[10], 71), 0)
    norm_gain = jnp.clip(1.0 + 0.1 * jax.random.normal(streams_of[3], (HEADS * P_SIZE,), jnp.float32), 0.5, 1.5)
    pool_down = noise(streams_of[4], (ADAPTERS, D, R), D ** -0.5, 0.078125, ((0, 8),))
    pool_up = noise(streams_of[5], (ADAPTERS, R, HEADS * P_SIZE), R ** -0.5, 0.75, ((0, 8),))
    span_id = draw_span_id(jax.random.fold_in(streams_of[10], 71), 0)
    prompt_adapter = touch_ends(jax.random.randint(streams_of[7], (PROMPTS,), 0, ADAPTERS), jax.random.fold_in(streams_of[7], 1), 0, ADAPTERS - 1).astype(jnp.int32)
    owner_pos = jax.random.permutation(streams_of[8], ADAPTERS).astype(jnp.int32)
    slice_len = draw_slice_len(jax.random.fold_in(streams_of[10], 71), 0)
    return {"tokens": tokens, "proj_weight": proj_weight, "decay_rate": decay_rate, "norm_gain": norm_gain, "pool_down": pool_down, "pool_up": pool_up, "span_id": span_id, "prompt_adapter": prompt_adapter, "owner_pos": owner_pos, "slice_len": slice_len}


NORM_FLOOR = 1.0

def slice_layer(rows, proj_weight, down_panel, up_panel, decay_rate, norm_gain, length, start_state):
    width = proj_weight.shape[2]
    heads = width // P_SIZE
    slot_ids = jnp.arange(SLICE, dtype=jnp.int32)
    causal = slot_ids[:, None] >= slot_ids[None, :]
    query = jnp.dot(rows, proj_weight[0], preferred_element_type=jnp.float32).astype(jnp.bfloat16)
    key_unprocessed = jnp.dot(rows, proj_weight[1], preferred_element_type=jnp.float32).astype(jnp.bfloat16)
    value = jnp.dot(rows, proj_weight[2], preferred_element_type=jnp.float32).astype(jnp.bfloat16)
    lower_rank_part = jnp.dot(rows, down_panel, preferred_element_type=jnp.float32).astype(jnp.bfloat16)
    gate = jnp.dot(rows, proj_weight[3], preferred_element_type=jnp.float32) + jnp.dot(lower_rank_part, up_panel, preferred_element_type=jnp.float32)
    live = (slot_ids < length).astype(jnp.float32)
    step_log = -(live[:, None] * decay_rate[None, :] * (2.0 * jax.nn.sigmoid(gate)))
    cumul = jnp.cumsum(step_log, axis=0).reshape(SLICE, heads, P_SIZE)
    query_f = query.astype(jnp.float32).reshape(SLICE, heads, P_SIZE)
    key_f = key_unprocessed.astype(jnp.float32).reshape(SLICE, heads, P_SIZE) * (live * P_SIZE ** (-0.5))[:, None, None]
    value_f = value.astype(jnp.float32).reshape(SLICE, heads, P_SIZE)
    query_decay = query_f * jnp.exp(cumul)
    key_decay = key_f * jnp.exp(-cumul)
    attention_scores = jnp.einsum('thc,jhc->htj', query_decay, key_decay, precision=lax.Precision.HIGHEST)
    attention_scores = jnp.where(causal[None], attention_scores, 0.0)
    inner = jnp.einsum('htj,jhd->thd', attention_scores, value_f, precision=lax.Precision.HIGHEST)
    inner = inner + jnp.einsum('thc,hcd->thd', query_decay, start_state, precision=lax.Precision.HIGHEST)
    normed = inner * lax.rsqrt(jnp.maximum(lax.optimization_barrier(jnp.mean(inner * inner, axis=-1, keepdims=True)), NORM_FLOOR)) * norm_gain.reshape(heads, P_SIZE)
    out_rows = (normed * live[:, None, None]).reshape(SLICE, width).astype(jnp.bfloat16)
    last_cumul = cumul[-1]
    carried = jnp.einsum('jhc,jhd->hcd', key_f * jnp.exp(last_cumul[None] - cumul), value_f, precision=lax.Precision.HIGHEST)
    end_state = jnp.exp(last_cumul)[:, :, None] * start_state + carried
    return (out_rows, end_state)

def reference(tokens, proj_weight, decay_rate, norm_gain, pool_down, pool_up, span_id, prompt_adapter, owner_pos, slice_len):
    width = proj_weight.shape[2]
    heads = width // P_SIZE

    def device_step(preceding_value, device_index):
        out_list = []
        state_list = []
        for lane_pos in range(LANES):
            prompt = span_id[device_index, lane_pos]
            earlier = span_id[jnp.maximum(device_index - 1, 0), lane_pos]
            keep_flag = jnp.where((device_index > 0) & (prompt == earlier), 1.0, 0.0).astype(jnp.float32)
            place = owner_pos[prompt_adapter[prompt]]
            offset = ((device_index * LANES + lane_pos) * SLICE).astype(jnp.int32)
            rows = lax.dynamic_slice_in_dim(tokens, offset, SLICE, 0)
            start_state = keep_flag * preceding_value[lane_pos]
            out_rows, end_state = slice_layer(rows, proj_weight, pool_down[place], pool_up[place], decay_rate, norm_gain, slice_len[device_index, lane_pos], start_state)
            out_list.append(out_rows)
            state_list.append(end_state)
        stacked = jnp.stack(state_list)
        return (stacked, (jnp.concatenate(out_list, axis=0), stacked.reshape(LANES, width, P_SIZE)))
    initial = jnp.zeros((LANES, heads, P_SIZE, P_SIZE), jnp.float32)
    _, (outs, states) = lax.scan(device_step, initial, jnp.arange(N_SEQ, dtype=jnp.int32))
    return (outs.reshape(N_SEQ * LANES * SLICE, width), states)
```

```python
import functools
import math

import jax
import jax.numpy as jnp
from jax import lax
from jax.experimental import pallas as pl
from jax.experimental.pallas import tpu as pltpu
from jax.sharding import PartitionSpec as P

P_SIZE = 128
NORM_FLOOR = 1.0
PIECES = 4
CHUNKS = 4
W_PARTS = 8
MESH = pl.DeviceIdType.MESH
HIGHEST = lax.Precision.HIGHEST


def grid_of(n):
    across = math.isqrt(n // 2)
    if across >= 2 and 2 * across * across == n:
        return across, n // across
    return 1, n


def head_at(position, n):
    across, depth = grid_of(n)
    if across == 1:
        return position
    width = across - 1
    back = lax.div(lax.div(position, depth) + (across - 1), across)
    rest = (position - depth) * back
    row, step = lax.div(rest, width), lax.rem(rest, width)
    x = 1 + step + lax.rem(row, 2) * (width - 1 - 2 * step)
    return (1 - back) * position * across + back * ((depth - 1 - row) * across + x)


def position_of(head, n):
    across, depth = grid_of(n)
    if across == 1:
        return head
    width = across - 1
    z, x = lax.div(head, across), lax.rem(head, across)
    back = lax.div(x + across - 1, across)
    row, step = depth - 1 - z, (x - 1) * back
    moved = step + lax.rem(row, 2) * (width - 1 - 2 * step)
    return (1 - back) * z + back * (depth + row * width + moved)


def dot(a, b, precision=None):
    return jnp.dot(a, b, preferred_element_type=jnp.float32, precision=precision)


def ring_kernel(
    n,
    n_seq,
    span_ref,
    prompt_ref,
    owner_ref,
    len_ref,
    tok_ref,
    w_hbm,
    down_hbm,
    up_ref,
    rate_ref,
    gain_ref,
    out_ref,
    state_ref,
    slots,
    wbuf,
    dbuf,
    dturn,
    acc,
    lacc,
    up_send,
    up_recv,
    low_send,
    low_recv,
    low_full,
    st_send,
    st_recv,
    w_sem,
    ring_send,
    ring_recv,
    up_ssem,
    up_rsem,
    rs_ssem,
    rs_rsem,
    ag_ssem,
    ag_rsem,
    st_ssem,
    st_rsem,
):
    me = lax.axis_index("head")
    seq = lax.axis_index("seq")
    rows, shard = tok_ref.shape
    lanes = span_ref.shape[0]
    per_owner = down_hbm.shape[0]
    rank = down_hbm.shape[1]
    slice_rows = rows // lanes
    piece = rows // PIECES
    half = n // 2
    here = position_of(me, n)
    right = head_at(lax.rem(here + 1, n), n)
    left = head_at(lax.rem(here + n - 1, n), n)
    toward = (right, left)

    loads = [
        pltpu.make_async_copy(w_hbm.at[c], wbuf.at[:, pl.ds(c * P_SIZE, P_SIZE)], w_sem.at[c])
        for c in range(4)
    ]
    loads.append(pltpu.make_async_copy(down_hbm, dturn, w_sem.at[4]))

    barrier = pltpu.get_barrier_semaphore()

    def greet_head(d, carry):
        pl.semaphore_signal(
            barrier, inc=1, device_id={"head": lax.rem(me + d, n)}, device_id_type=MESH
        )
        return carry

    def greet_seq(d, carry):
        pl.semaphore_signal(
            barrier, inc=1, device_id={"seq": lax.rem(seq + d, n_seq)}, device_id_type=MESH
        )
        return carry

    lax.fori_loop(1, n, greet_head, 0)
    lax.fori_loop(1, n_seq, greet_seq, 0)
    for load in loads:
        load.start()
    pl.semaphore_wait(barrier, n - 1 + n_seq - 1)

    def hop(direction, step, p, own=False):
        span = pl.ds(p * piece, piece)
        source = tok_ref.at[span] if own else slots.at[direction, step - 2, span]
        return pltpu.make_async_remote_copy(
            src_ref=source,
            dst_ref=slots.at[direction, step - 1, span],
            send_sem=ring_send.at[direction, step - 1, p],
            recv_sem=ring_recv.at[direction, step - 1, p],
            device_id={"head": toward[direction]},
            device_id_type=MESH,
        )

    def long_way(direction, p):
        return p % 2 == direction

    for k in range(PIECES):
        for direction in range(2):
            hop(direction, 1, (k + direction) % PIECES, own=True).start()

    places = [owner_ref[prompt_ref[span_ref[j, seq]]] for j in range(lanes)]
    owned = [
        [jnp.where(places[j] == me * per_owner + s, 1.0, 0.0).astype(jnp.float32) for s in range(per_owner)]
        for j in range(lanes)
    ]

    for j in range(lanes):
        mine = sum(owned[j][s] * up_ref[s].astype(jnp.float32) for s in range(per_owner)).astype(jnp.bfloat16)
        for i in range(n):
            up_send[i, pl.ds(j * rank, rank), :] = mine[:, i * P_SIZE : (i + 1) * P_SIZE]

    def up_copy(d):
        peer = lax.rem(me + d, n)
        return pltpu.make_async_remote_copy(
            src_ref=up_send.at[peer],
            dst_ref=up_recv.at[d],
            send_sem=up_ssem.at[d],
            recv_sem=up_rsem.at[d],
            device_id={"head": peer},
            device_id_type=MESH,
        )

    def up_start(d, carry):
        up_copy(d).start()
        return carry

    lax.fori_loop(1, n, up_start, 0)
    up_recv[0] = up_send[me]

    for load in loads:
        load.wait()

    strip = wbuf.shape[0] // 12

    def turn_strip(i, carry):
        deep = pl.ds(pl.multiple_of(i * strip, strip), strip)
        for s in range(per_owner):
            dbuf[s, deep, :] = dturn[s, :, deep].T
        return carry

    lax.fori_loop(0, 12, turn_strip, 0)

    def multiply(x, span, origin, first=False):
        deep = pl.ds(pl.multiple_of(origin * shard, 64), shard)
        gained = dot(x, wbuf[deep, :])
        lows = [dot(x, dbuf[s, deep, :]) for s in range(per_owner)]
        if first:
            acc[span, :] = gained
            for s in range(per_owner):
                lacc[s, span, :] = lows[s]
        else:
            acc[span, :] += gained
            for s in range(per_owner):
                lacc[s, span, :] += lows[s]

    def own_piece(p, carry):
        span = pl.ds(pl.multiple_of(p * piece, piece), piece)
        multiply(tok_ref[span, :], span, me, first=True)
        return carry

    lax.fori_loop(0, PIECES, own_piece, 0)

    def arrive(step, forward, present):
        order = [((k + d) % PIECES, d) for k in range(PIECES) for d in range(2)]
        order = [(p, d) for p, d in order if present(d, p)]
        for p, d in order:
            hop(d, step, p).wait_recv() if not isinstance(step, int) or step > 1 else hop(d, 1, p, own=True).wait_recv()
            if forward(d, p):
                hop(d, step + 1, p).start()
            sign = n - step if d == 0 else step
            origin = head_at(lax.rem(here + sign, n), n)
            span = pl.ds(p * piece, piece)
            multiply(slots[d, step - 1, span, :], span, origin)

    everything = lambda d, p: True
    nothing = lambda d, p: False
    if half >= 2:
        arrive(1, everything if half > 2 else long_way, everything)
    if half > 3:

        def middle(step, carry):
            arrive(step, everything, everything)
            return carry

        lax.fori_loop(2, half - 1, middle, 0)
    if half > 2:
        arrive(half - 1, long_way, everything)
    arrive(half, nothing, long_way)

    width = lanes * rank
    for j in range(lanes):
        span = pl.ds(j * slice_rows, slice_rows)
        mine = sum(owned[j][s] * lacc[s, span, :] for s in range(per_owner)).astype(jnp.bfloat16)
        low_send[:, pl.ds(j * rank, rank)] = mine
    block = slice_rows // n

    def rs_copy(d):
        peer = lax.rem(me + d, n)
        return pltpu.make_async_remote_copy(
            src_ref=low_send.at[pl.ds(pl.multiple_of(peer * block, block), block)],
            dst_ref=low_recv.at[d],
            send_sem=rs_ssem.at[d],
            recv_sem=rs_rsem.at[d],
            device_id={"head": peer},
            device_id_type=MESH,
        )

    def ag_copy(d):
        peer = lax.rem(me + d, n)
        return pltpu.make_async_remote_copy(
            src_ref=low_recv.at[0],
            dst_ref=low_full.at[me],
            send_sem=ag_ssem.at[d],
            recv_sem=ag_rsem.at[d],
            device_id={"head": peer},
            device_id_type=MESH,
        )

    def ag_arrival(d):
        peer = lax.rem(me + n - d, n)
        return pltpu.make_async_remote_copy(
            src_ref=low_recv.at[0],
            dst_ref=low_full.at[peer],
            send_sem=ag_ssem.at[d],
            recv_sem=ag_rsem.at[d],
            device_id={"head": peer},
            device_id_type=MESH,
        )

    def each(count, act):
        def turn(d, carry):
            act(d)
            return carry

        lax.fori_loop(1, count, turn, 0)

    each(n, lambda d: rs_copy(d).start())
    each(n, lambda d: up_copy(d).wait_recv())
    up = jnp.sum(up_recv[...].astype(jnp.float32), axis=0).astype(jnp.bfloat16)
    total = low_send[pl.ds(pl.multiple_of(me * block, block), block), :].astype(jnp.float32)
    each(n, lambda d: rs_copy(d).wait_recv())
    for d in range(1, n):
        total = total + low_recv[d].astype(jnp.float32)
    low_recv[0] = total.astype(jnp.bfloat16)
    each(n, lambda d: ag_copy(d).start())
    low_full[me] = total.astype(jnp.bfloat16)

    slot_ids = lax.broadcasted_iota(jnp.int32, (slice_rows, 1), 0)
    causal = lax.broadcasted_iota(jnp.int32, (slice_rows, slice_rows), 0) >= lax.broadcasted_iota(
        jnp.int32, (slice_rows, slice_rows), 1
    )
    triangle = jnp.where(causal, 1.0, 0.0).astype(jnp.float32)
    columns = lax.broadcasted_iota(jnp.int32, (1, width), 1)
    each(n, lambda d: ag_arrival(d).wait_recv())
    low = low_full[...].reshape(slice_rows, width).astype(jnp.float32)

    kept = []
    for j in range(lanes):
        span = pl.ds(j * slice_rows, slice_rows)
        own = (columns >= j * rank) & (columns < (j + 1) * rank)
        gate = acc[span, pl.ds(3 * P_SIZE, P_SIZE)] + dot(jnp.where(own, low, 0.0).astype(jnp.bfloat16), up)
        live = jnp.where(slot_ids < len_ref[j, seq], 1.0, 0.0).astype(jnp.float32)
        step_log = -(live * rate_ref[...] * (2.0 * jax.nn.sigmoid(gate)))
        cumul = dot(triangle, step_log, HIGHEST)
        query = acc[span, pl.ds(0, P_SIZE)].astype(jnp.bfloat16).astype(jnp.float32)
        key = acc[span, pl.ds(P_SIZE, P_SIZE)].astype(jnp.bfloat16).astype(jnp.float32) * (
            live * P_SIZE ** (-0.5)
        )
        value = acc[span, pl.ds(2 * P_SIZE, P_SIZE)].astype(jnp.bfloat16).astype(jnp.float32)
        last = cumul[slice_rows - 1 :, :]
        carried = lax.dot_general(
            key * jnp.exp(last - cumul),
            value,
            (((0,), (0,)), ((), ())),
            precision=HIGHEST,
            preferred_element_type=jnp.float32,
        )
        st_send[j, pl.ds(0, P_SIZE), :] = carried
        st_send[j, pl.ds(P_SIZE, 8), :] = jnp.broadcast_to(jnp.exp(last), (8, P_SIZE))
        kept.append((live, query * jnp.exp(cumul), key * jnp.exp(-cumul), value))

    def st_copy(d):
        return pltpu.make_async_remote_copy(
            src_ref=st_send,
            dst_ref=st_recv.at[seq],
            send_sem=st_ssem.at[d],
            recv_sem=st_rsem.at[d],
            device_id={"seq": lax.rem(seq + d, n_seq)},
            device_id_type=MESH,
        )

    def st_arrival(d):
        peer = lax.rem(seq + n_seq - d, n_seq)
        return pltpu.make_async_remote_copy(
            src_ref=st_send,
            dst_ref=st_recv.at[peer],
            send_sem=st_ssem.at[d],
            recv_sem=st_rsem.at[d],
            device_id={"seq": peer},
            device_id_type=MESH,
        )

    each(n_seq, lambda d: st_copy(d).start())
    st_recv[seq] = st_send[...]

    inners = []
    for j in range(lanes):
        live, query_decay, key_decay, value = kept[j]
        scores = lax.dot_general(
            query_decay,
            key_decay,
            (((1,), (1,)), ((), ())),
            precision=HIGHEST,
            preferred_element_type=jnp.float32,
        )
        inners.append(dot(jnp.where(causal, scores, 0.0), value, HIGHEST))

    each(n_seq, lambda d: st_arrival(d).wait_recv())
    for j in range(lanes):
        live, query_decay, _, _ = kept[j]
        span = pl.ds(j * slice_rows, slice_rows)
        ended = jnp.zeros((P_SIZE, P_SIZE), jnp.float32)
        start = ended
        final = ended
        for k in range(n_seq):
            if k:
                same = jnp.where(span_ref[j, k] == span_ref[j, k - 1], 1.0, 0.0).astype(jnp.float32)
                begun = same * ended
            else:
                begun = ended
            decay = jnp.broadcast_to(st_recv[k, j, pl.ds(P_SIZE, 1), :], (P_SIZE, P_SIZE)).T
            ended = decay * begun + st_recv[k, j, pl.ds(0, P_SIZE), :]
            at = jnp.where(seq == k, 1.0, 0.0).astype(jnp.float32)
            start = start + at * begun
            final = final + at * ended
        inner = inners[j] + dot(query_decay, start, HIGHEST)
        scale = lax.rsqrt(jnp.maximum(jnp.mean(inner * inner, axis=-1, keepdims=True), NORM_FLOOR))
        out_ref[span, :] = (inner * scale * gain_ref[...] * live).astype(jnp.bfloat16)
        state_ref[0, j] = final

    each(n, lambda d: up_copy(d).wait_send())
    each(n, lambda d: rs_copy(d).wait_send())
    each(n, lambda d: ag_copy(d).wait_send())
    each(n_seq, lambda d: st_copy(d).wait_send())
    for p in range(PIECES):
        for direction in range(2):
            hop(direction, 1, p, own=True).wait_send()
    for direction in range(2):
        for p in range(PIECES):
            reach = half if long_way(direction, p) else half - 1

            def drained(step, carry):
                hop(direction, step, p).wait_send()
                return carry

            lax.fori_loop(2, reach + 1, drained, 0)


def halves(a):
    high = a.astype(jnp.bfloat16)
    return high, (a - high.astype(jnp.float32)).astype(jnp.bfloat16)


def across_rows(a, b):
    return lax.dot_general(a, b, (((1,), (1,)), ((), ())), preferred_element_type=jnp.float32)


def down_rows(a, b):
    return lax.dot_general(a, b, (((0,), (0,)), ((), ())), preferred_element_type=jnp.float32)


def paired_kernel(
    span_ref,
    prompt_ref,
    owner_ref,
    len_ref,
    tok_ref,
    w_hbm,
    down_hbm,
    up_ref,
    rate_ref,
    gain_ref,
    out_ref,
    state_ref,
    tokbuf,
    wbuf,
    dturn,
    dsend,
    din,
    dbuf,
    acc,
    lacc,
    lowb,
    upsend,
    upin,
    upsum,
    upr,
    rgbuf,
    qdh,
    qdl,
    inn,
    run,
    carry,
    st_send,
    st_recv,
    obuf,
    fbuf,
    w_sem,
    t_local,
    t_send,
    t_recv,
    f_send,
    wz_send,
    wz_recv,
    wy_send,
    wy_recv,
    wc_send,
    wc_recv,
    r_send,
    r_recv,
    p_send,
    p_recv,
    u_send,
    u_recv,
    l_send,
    l_recv,
    s_send,
    s_recv,
    o_send,
    o_recv,
    e_send,
    e_recv,
    o_local,
):
    h = lax.axis_index("head")
    s = lax.axis_index("seq")
    z, x = lax.div(h, 2), lax.rem(h, 2)
    y, k = lax.div(s, 2), lax.rem(s, 2)
    b, p = lax.div(z, 2), lax.rem(z, 2)
    zi, z2, z3 = z + 1 - 2 * p, lax.rem(z + 2, 4), 3 - z
    same = k == p
    differ = k != p
    inner = (z == 1) | (z == 2)
    outer = (z == 0) | (z == 3)
    inward = 1 + p
    seqc = 2 * y + p
    lane = k

    rows, shard = tok_ref.shape
    lanes = span_ref.shape[0]
    per_owner, rank, model = down_hbm.shape
    slice_rows = rows // lanes
    chunk = slice_rows // CHUNKS
    deep_part = model // W_PARTS
    wide = 4 * P_SIZE

    def at(xx, yy, zz, kk):
        return {"head": 2 * zz + xx, "seq": 2 * yy + kk}

    def remote(src, dst, send, recv, where):
        return pltpu.make_async_remote_copy(
            src_ref=src, dst_ref=dst, send_sem=send, recv_sem=recv, device_id=where, device_id_type=MESH
        )

    loads = [
        pltpu.make_async_copy(
            w_hbm.at[c],
            wbuf.at[:, pl.ds(pl.multiple_of(p * wide + c * P_SIZE, P_SIZE), P_SIZE)],
            w_sem.at[c],
        )
        for c in range(4)
    ]
    pools = pltpu.make_async_copy(down_hbm, dturn, w_sem.at[4])

    barrier = pltpu.get_barrier_semaphore()
    plane = 2 * h + k

    def greet(d, c):
        other = lax.rem(plane + d, 16)
        where = {"head": lax.div(other, 2), "seq": 2 * y + lax.rem(other, 2)}
        pl.semaphore_signal(barrier, inc=1, device_id=where, device_id_type=MESH)
        return c

    lax.fori_loop(1, 16, greet, 0)
    for zz in (z, zi):
        pl.semaphore_signal(barrier, inc=1, device_id=at(x, 1 - y, zz, k), device_id_type=MESH)
    pools.start()
    rgbuf[p, pl.ds(0, 1), :] = rate_ref[...]
    rgbuf[p, pl.ds(1, 1), :] = gain_ref[...]
    pl.semaphore_wait(barrier, 17)

    def deep_at(i):
        return pl.ds(pl.multiple_of(i * deep_part, 128), deep_part)

    def col_at(q, c):
        return pl.ds(pl.multiple_of(q * wide + c * P_SIZE, P_SIZE), P_SIZE)

    def wz_copy(i):
        c = 2 * y + k
        return remote(
            w_hbm.at[c, deep_at(i)],
            wbuf.at[deep_at(i), col_at(p, c)],
            wz_send.at[i],
            wz_recv.at[i],
            at(x, y, zi, k),
        )

    def held(i, c):
        return wbuf.at[deep_at(i), col_at(1 - p, c)]

    def wz_arrival(i):
        c = 2 * y + k
        return remote(held(i, c), held(i, c), wz_send.at[i], wz_recv.at[i], at(x, y, zi, k))

    def wy_copy(i):
        c = 2 * y + k
        return remote(held(i, c), held(i, c), wy_send.at[i], wy_recv.at[i], at(x, 1 - y, z, k))

    def wy_arrival(i):
        c = 2 * (1 - y) + k
        return remote(held(i, c), held(i, c), wy_send.at[i], wy_recv.at[i], at(x, 1 - y, z, k))

    def wc_copy(g, i):
        c = 2 * (y + g - 2 * y * g) + k
        return remote(held(i, c), held(i, c), wc_send.at[g, i], wc_recv.at[g, i], at(x, y, z, 1 - k))

    def wc_arrival(g, i):
        c = 2 * (y + g - 2 * y * g) + 1 - k
        return remote(held(i, c), held(i, c), wc_send.at[g, i], wc_recv.at[g, i], at(x, y, z, 1 - k))

    def each(first, count, act):
        def turn(i, c):
            act(i)
            return c

        lax.fori_loop(first, count, turn, 0)

    each(0, W_PARTS, lambda i: wz_copy(i).start())
    for load in loads:
        load.start()

    rg_copy = remote(rgbuf.at[p], rgbuf.at[p], r_send, r_recv, at(x, y, zi, k))
    rg_arrival = remote(rgbuf.at[1 - p], rgbuf.at[1 - p], r_send, r_recv, at(x, y, zi, k))
    rg_copy.start()

    def chunk_at(r):
        return pl.ds(pl.multiple_of(r * chunk, chunk), chunk)

    def place(f, r):
        return tokbuf.at[chunk_at(r), pl.ds(pl.multiple_of(f * shard, 128), shard)]

    def tok_copy(t, j, r, where):
        source = tok_ref.at[pl.ds(pl.multiple_of(j * slice_rows + r * chunk, chunk), chunk)]
        return remote(source, place(h, r), t_send.at[t, j, r], t_recv.at[h, r], where)

    def free_sends(r, act):
        @pl.when(same)
        def _():
            act(tok_copy(0, 1 - k, r, at(x, y, z, 1 - k)))
            for j in range(2):
                act(tok_copy(1, j, r, at(1 - x, y, z, j)))

        @pl.when(differ & inner)
        def _():
            for j in range(2):
                act(tok_copy(2, j, r, at(x, y, z3, j)))

    def late_sends(r, act):
        @pl.when(same)
        def _():
            for j in range(2):
                act(tok_copy(2, j, r, at(x, y, z2, j)))

        @pl.when(differ)
        def _():
            for j in range(2):
                act(tok_copy(1, j, r, at(x, y, zi, j)))

    own = pltpu.make_async_copy(
        tok_ref.at[pl.ds(pl.multiple_of(lane * slice_rows, chunk), slice_rows)],
        tokbuf.at[:, pl.ds(pl.multiple_of(h * shard, 128), shard)],
        t_local,
    )

    each(0, CHUNKS, lambda r: free_sends(r, lambda copy: copy.start()))

    @pl.when(same)
    def _():
        own.start()

    def mask(seq):
        spot = owner_ref[prompt_ref[span_ref[lane, seq]]]
        return [jnp.where(spot == h * per_owner + i, 1.0, 0.0).astype(jnp.float32) for i in range(per_owner)]

    mine, theirs = mask(seqc), mask(2 * y + 1 - p)
    pools.wait()
    strips = 12
    strip = model // strips

    def strip_at(i):
        return pl.ds(pl.multiple_of(i * strip, 128), strip)

    def pick(weights, i):
        return sum(weights[o] * dturn[o, :, strip_at(i)].astype(jnp.float32) for o in range(per_owner))

    def fill_send(i):
        dsend[:, strip_at(i)] = pick(theirs, i).astype(jnp.bfloat16)

    each(0, strips, fill_send)
    for g in range(4):
        for q in range(2):
            head = 4 * (g // 2) + 2 * q + g % 2
            part = [up_ref[o, :, head * P_SIZE : (head + 1) * P_SIZE].astype(jnp.float32) for o in range(per_owner)]
            upsend[g, q] = sum(theirs[o] * part[o] for o in range(per_owner)).astype(jnp.bfloat16)
            upsum[g, q] = sum(mine[o] * part[o] for o in range(per_owner)).astype(jnp.bfloat16)

    from_outer = jnp.where(inner, 1, 0)
    pan_copy = remote(dsend, din.at[from_outer], p_send.at[0], p_recv.at[from_outer], at(x, y, inward, k))
    upp_copy = remote(upsend, upin.at[from_outer], p_send.at[1], p_recv.at[2 + from_outer], at(x, y, inward, k))

    def arrived(f, r):
        remote(place(f, r), place(f, r), t_send.at[0, 0, 0], t_recv.at[f, r], at(1 - x, y, z, k)).wait_recv()

    def x_forward(a, zz, r):
        f = 2 * zz + x
        return remote(place(f, r), place(f, r), f_send.at[a - 1, r], t_recv.at[f, r], at(1 - x, y, z, k))

    def z_forward(r):
        f = 2 * zi + x
        return remote(place(f, r), place(f, r), f_send.at[3, r], t_recv.at[f, r], at(x, y, z2, k))

    @pl.when(inner)
    def _():
        pan_copy.start()
        upp_copy.start()

    def spread(i, c):
        wz_arrival(i).wait_recv()
        wy_copy(i).start()
        wc_copy(0, i).start()

        @pl.when(i > 0)
        def _():
            wy_arrival(i - 1).wait_recv()
            wc_copy(1, i - 1).start()

        @pl.when(inner & (lax.rem(i, W_PARTS // CHUNKS) == W_PARTS // CHUNKS - 1))
        def _():
            r = lax.div(i, W_PARTS // CHUNKS)
            arrived(2 * z3 + x, r)
            x_forward(3, z3, r).start()

        @pl.when((i == W_PARTS - 1) & outer)
        def _():
            pan_copy.start()
            upp_copy.start()

        @pl.when(i == W_PARTS - 1)
        def _():
            each(0, CHUNKS, lambda r: late_sends(r, lambda copy: copy.start()))

        return c

    lax.fori_loop(0, W_PARTS, spread, 0)
    wy_arrival(W_PARTS - 1).wait_recv()
    wc_copy(1, W_PARTS - 1).start()

    @pl.when(inner)
    def _():
        for g in range(2):
            remote(dsend, din.at[g], p_send.at[0], p_recv.at[g], at(x, y, zi, k)).wait_recv()
            remote(upsend, upin.at[g], p_send.at[1], p_recv.at[2 + g], at(x, y, zi, k)).wait_recv()

        def turn(i):
            whole = pick(mine, i)
            for g in range(2):
                whole = whole + din[g, :, strip_at(i)].astype(jnp.float32)
            dbuf[strip_at(i), :rank] = whole.astype(jnp.bfloat16).T
            dbuf[strip_at(i), rank:] = jnp.zeros((strip, P_SIZE - rank), jnp.bfloat16)

        each(0, strips, turn)
        whole = upsum[...].astype(jnp.float32)
        for g in range(2):
            whole = whole + upin[g].astype(jnp.float32)
        upsum[...] = whole.astype(jnp.bfloat16)

    @pl.when(outer)
    def _():
        def turn(i):
            dbuf[strip_at(i), :rank] = pick(mine, i).astype(jnp.bfloat16).T
            dbuf[strip_at(i), rank:] = jnp.zeros((strip, P_SIZE - rank), jnp.bfloat16)

        each(0, strips, turn)

    mates = [None, at(1 - x, y, z, k), at(x, y, z2, k), at(1 - x, y, z2, k)]
    groups = [2 * b + x, 2 * b + 1 - x, 2 * (1 - b) + x, 2 * (1 - b) + 1 - x]

    def up_copy(d):
        return remote(upsum.at[groups[d]], upr.at[d], u_send.at[d], u_recv.at[d], mates[d])

    for d in range(1, 4):
        up_copy(d).start()
    upr[0] = upsum[groups[0]]

    def low_copy(d, r):
        return remote(lowb.at[0, chunk_at(r)], lowb.at[d, chunk_at(r)], l_send.at[d, r], l_recv.at[d, r], mates[d])

    run[...] = jnp.zeros_like(run)
    carry[...] = jnp.zeros_like(carry)

    def shard_of(a, column):
        high, bit = lax.div(a, 2), lax.rem(a, 2)
        zz = 2 * (b + high - 2 * b * high) + p + bit - 2 * p * bit
        return 2 * zz + column

    def multiply(f, r, first):
        span = chunk_at(r)
        deep = pl.ds(pl.multiple_of(f * shard, 128), shard)
        block = tokbuf[span, deep]
        low_part = dot(block, dbuf[deep, :])
        part = dot(block, wbuf[deep, :])

        @pl.when(first)
        def _():
            lacc[...] = low_part
            acc[span, :] = part

        @pl.when(jnp.logical_not(first))
        def _():
            lacc[...] += low_part
            acc[span, :] += part

    def onward(a, zz, r):
        arrived(2 * zz + x, r)
        x_forward(a, zz, r).start()

    def advance(r):
        @pl.when(inner)
        def _():
            onward(1, zi, r)
            z_forward(r).start()
            onward(2, z2, r)

        @pl.when(outer)
        def _():
            onward(3, z3, r)

            @pl.when(r + 2 < CHUNKS)
            def _():
                onward(1, zi, r + 2)

        @pl.when(differ)
        def _():
            arrived(h, r)

        @pl.when(same & (r == 0))
        def _():
            own.wait()

    soon = jnp.where(inner, 3, 2)

    def other(a, r):
        f = shard_of(a, 1 - x)
        arrived(f, r)
        multiply(f, r, a < 0)

    def early(r):
        each(0, 4, lambda a: multiply(shard_of(a, x), r, a == 0))
        each(0, 2, lambda i: other(i * soon, r))

    def finish(r):
        second, step_to = jnp.where(inner, 2, 1), jnp.where(inner, -1, 2)
        each(0, 2, lambda i: other(second + i * step_to, r))
        lowb[0, chunk_at(r), :] = lacc[...].astype(jnp.bfloat16)
        for d in range(1, 4):
            low_copy(d, r).start()

    row_ids = lax.broadcasted_iota(jnp.int32, (chunk, chunk), 0)
    column_ids = lax.broadcasted_iota(jnp.int32, (chunk, chunk), 1)
    causal = row_ids >= column_ids
    triangle = jnp.where(causal, 1.0, 0.0).astype(jnp.bfloat16)
    slot_ids = lax.broadcasted_iota(jnp.int32, (slice_rows, 1), 0)
    chunk_ids = lax.broadcasted_iota(jnp.int32, (chunk, 1), 0)
    length = len_ref[lane, seqc]

    def state_copy(d):
        where = [None, at(x, 1 - y, z, k), at(x, y, zi, k), at(x, 1 - y, zi, k)][d]
        return remote(st_send, st_recv.at[seqc], s_send.at[d], s_recv.at[d], where)

    def state_arrival(d):
        yy, pp = [None, (1 - y, p), (y, 1 - p), (1 - y, 1 - p)][d]
        return remote(st_send, st_recv.at[2 * yy + pp], s_send.at[d], s_recv.at[d], at(x, 1 - y, z, k))

    def attend(r):
        span = chunk_at(r)

        @pl.when(r == 0)
        def _():
            for d in range(1, 4):
                up_copy(d).wait_recv()
            for q in range(2):
                upr[0, q] = sum(upr[d, q].astype(jnp.float32) for d in range(4)).astype(jnp.bfloat16)

        for d in range(1, 4):
            low_copy(d, r).wait_recv()
        low = sum(lowb[d, span, :].astype(jnp.float32) for d in range(4)).astype(jnp.bfloat16)
        live = jnp.where(chunk_ids + r * chunk < length, 1.0, 0.0).astype(jnp.float32)
        kept = []
        for q in range(2):
            first = q * wide
            gate = acc[span, first + 3 * P_SIZE : first + 4 * P_SIZE] + dot(low[:, :rank], upr[0, q])
            step_log = -(live * rgbuf[q, pl.ds(0, 1), :] * (2.0 * jax.nn.sigmoid(gate)))
            a0, rest = halves(step_log)[0], step_log
            rest = rest - a0.astype(jnp.float32)
            a1, a2 = halves(rest)
            cumul = dot(triangle, a0) + (dot(triangle, a1) + dot(triangle, a2)) + carry[q, pl.ds(0, 1), :]
            carry[q] = jnp.broadcast_to(cumul[chunk - 1 :, :], (8, P_SIZE))
            query = acc[span, first : first + P_SIZE].astype(jnp.bfloat16).astype(jnp.float32)
            key = acc[span, first + P_SIZE : first + 2 * P_SIZE].astype(jnp.bfloat16).astype(jnp.float32) * (
                live * P_SIZE ** (-0.5)
            )
            value = acc[span, first + 2 * P_SIZE : first + 3 * P_SIZE].astype(jnp.bfloat16)
            q_high, q_low = halves(query * jnp.exp(cumul))
            k_high, k_low = halves(key * jnp.exp(-cumul))
            qdh[q, span, :] = q_high
            qdl[q, span, :] = q_low
            before = run[q]
            run[q] = before + (down_rows(k_high, value) + down_rows(k_low, value))
            kept.append((q_high, q_low, k_high, k_low, value, before))

        @pl.when(r == CHUNKS - 1)
        def _():
            for q in range(2):
                st_send[q, pl.ds(0, P_SIZE), :] = run[q]
                st_send[q, pl.ds(P_SIZE, 8), :] = jnp.exp(carry[q])
            for d in range(1, 4):
                state_copy(d).start()
            st_recv[seqc] = st_send[...]

        for q in range(2):
            q_high, q_low, k_high, k_low, value, before = kept[q]
            scores = across_rows(q_high, k_high) + (across_rows(q_high, k_low) + across_rows(q_low, k_high))
            s_high, s_low = halves(jnp.where(causal, scores, 0.0))
            b_high, b_low = halves(before)
            inn[q, span, :] = (
                dot(s_high, value)
                + dot(s_low, value)
                + dot(q_high, b_high)
                + (dot(q_high, b_low) + dot(q_low, b_high))
            )

    @pl.when(outer)
    def _():
        each(0, CHUNKS, lambda r: onward(2, z2, r))
        each(0, 2, lambda r: onward(1, zi, r))

    for i in range(4):
        loads[i].wait()
    each(0, W_PARTS, lambda i: wc_arrival(0, i).wait_recv())
    each(0, W_PARTS, lambda i: wc_arrival(1, i).wait_recv())
    rg_arrival.wait_recv()
    def step(t, c):
        @pl.when(t < CHUNKS)
        def _():
            advance(t)

        @pl.when((t > 0) & (t <= CHUNKS))
        def _():
            finish(t - 1)

        @pl.when(t < CHUNKS)
        def _():
            early(t)

        @pl.when(t > 1)
        def _():
            attend(t - 2)

        return c

    lax.fori_loop(0, CHUNKS + 2, step, 0)

    for d in range(1, 4):
        state_arrival(d).wait_recv()
    alive = jnp.where(slot_ids < length, 1.0, 0.0).astype(jnp.float32)

    def out_copy(q, where):
        return remote(
            obuf.at[q],
            out_ref.at[pl.ds(pl.multiple_of(lane * slice_rows, chunk), slice_rows)],
            o_send.at[q],
            o_recv.at[lane],
            where,
        )

    def end_copy(q, where):
        return remote(fbuf.at[q], state_ref.at[0, lane], e_send.at[q], e_recv.at[lane], where)

    keep_out = pltpu.make_async_copy(
        obuf.at[p], out_ref.at[pl.ds(pl.multiple_of(lane * slice_rows, chunk), slice_rows)], o_local.at[0]
    )
    keep_end = pltpu.make_async_copy(fbuf.at[p], state_ref.at[0, lane], o_local.at[1])
    away, beside = at(x, y, zi, p), at(x, y, z, 1 - k)

    for i in range(2):
        q = 1 - p if i == 0 else p
        ended = jnp.zeros((P_SIZE, P_SIZE), jnp.float32)
        start = ended
        final = ended
        for g in range(4):
            if g:
                kin = jnp.where(span_ref[lane, g] == span_ref[lane, g - 1], 1.0, 0.0).astype(jnp.float32)
                begun = kin * ended
            else:
                begun = ended
            decay = jnp.broadcast_to(st_recv[g, q, pl.ds(P_SIZE, 1), :], (P_SIZE, P_SIZE)).T
            ended = decay * (begun + st_recv[g, q, pl.ds(0, P_SIZE), :])
            now = jnp.where(seqc == g, 1.0, 0.0).astype(jnp.float32)
            start = start + now * begun
            final = final + now * ended
        fbuf[q] = final
        b_high, b_low = halves(start)
        total = inn[q] + dot(qdh[q], b_high) + (dot(qdh[q], b_low) + dot(qdl[q], b_high))
        scale = lax.rsqrt(jnp.maximum(jnp.mean(total * total, axis=-1, keepdims=True), NORM_FLOOR))
        obuf[q] = (total * scale * rgbuf[q, pl.ds(1, 1), :] * alive).astype(jnp.bfloat16)
        if i == 0:
            end_copy(q, away).start()
            out_copy(q, away).start()
        else:

            @pl.when(same)
            def _():
                keep_end.start()
                keep_out.start()

            @pl.when(differ)
            def _():
                end_copy(p, beside).start()
                out_copy(p, beside).start()

    def landed(j):
        span = pl.ds(pl.multiple_of(j * slice_rows, chunk), slice_rows)
        remote(obuf.at[0], out_ref.at[span], o_send.at[0], o_recv.at[j], beside).wait_recv()
        remote(fbuf.at[0], state_ref.at[0, j], e_send.at[0], e_recv.at[j], beside).wait_recv()

    landed(1 - k)

    @pl.when(same)
    def _():
        keep_end.wait()
        keep_out.wait()

    @pl.when(differ)
    def _():
        landed(k)
        end_copy(p, beside).wait_send()
        out_copy(p, beside).wait_send()

    end_copy(1 - p, away).wait_send()
    out_copy(1 - p, away).wait_send()
    each(0, W_PARTS, lambda i: wz_copy(i).wait_send())
    each(0, W_PARTS, lambda i: wy_copy(i).wait_send())
    each(0, W_PARTS, lambda i: wc_copy(0, i).wait_send())
    each(0, W_PARTS, lambda i: wc_copy(1, i).wait_send())
    rg_copy.wait_send()
    pan_copy.wait_send()
    upp_copy.wait_send()
    for d in range(1, 4):
        up_copy(d).wait_send()
        state_copy(d).wait_send()

    def drained(r):
        free_sends(r, lambda copy: copy.wait_send())
        late_sends(r, lambda copy: copy.wait_send())
        for a, zz in ((1, zi), (2, z2), (3, z3)):
            x_forward(a, zz, r).wait_send()

        @pl.when(inner)
        def _():
            z_forward(r).wait_send()

        for d in range(1, 4):
            low_copy(d, r).wait_send()

    each(0, CHUNKS, drained)


def paired_call(args):
    tokens, proj_weight, decay_rate, norm_gain, pool_down, pool_up, span_id, prompt_adapter, owner_pos, slice_len = args
    rows, shard = tokens.shape
    model = proj_weight.shape[1]
    lanes = span_id.shape[1]
    per_owner, _, rank = pool_down.shape
    slice_rows = rows // lanes
    smem = pl.BlockSpec(memory_space=pltpu.SMEM)
    vmem = pl.BlockSpec(memory_space=pltpu.VMEM)
    hbm = pl.BlockSpec(memory_space=pl.ANY)
    dma = pltpu.SemaphoreType.DMA
    bf16, f32 = jnp.bfloat16, jnp.float32
    chunk = slice_rows // CHUNKS
    return pl.pallas_call(
        paired_kernel,
        out_shape=(
            jax.ShapeDtypeStruct((rows, P_SIZE), bf16),
            jax.ShapeDtypeStruct((1, lanes, P_SIZE, P_SIZE), f32),
        ),
        in_specs=[smem, smem, smem, smem, vmem, hbm, hbm, vmem, vmem, vmem],
        out_specs=(vmem, vmem),
        scratch_shapes=[
            pltpu.VMEM((slice_rows, model), bf16),
            pltpu.VMEM((model, 8 * P_SIZE), bf16),
            pltpu.VMEM((per_owner, rank, model), bf16),
            pltpu.VMEM((rank, model), bf16),
            pltpu.VMEM((2, rank, model), bf16),
            pltpu.VMEM((model, P_SIZE), bf16),
            pltpu.VMEM((slice_rows, 8 * P_SIZE), f32),
            pltpu.VMEM((chunk, P_SIZE), f32),
            pltpu.VMEM((4, slice_rows, P_SIZE), bf16),
            pltpu.VMEM((4, 2, rank, P_SIZE), bf16),
            pltpu.VMEM((2, 4, 2, rank, P_SIZE), bf16),
            pltpu.VMEM((4, 2, rank, P_SIZE), bf16),
            pltpu.VMEM((4, 2, rank, P_SIZE), bf16),
            pltpu.VMEM((2, 8, P_SIZE), f32),
            pltpu.VMEM((2, slice_rows, P_SIZE), bf16),
            pltpu.VMEM((2, slice_rows, P_SIZE), bf16),
            pltpu.VMEM((2, slice_rows, P_SIZE), f32),
            pltpu.VMEM((2, P_SIZE, P_SIZE), f32),
            pltpu.VMEM((2, 8, P_SIZE), f32),
            pltpu.VMEM((2, P_SIZE + 8, P_SIZE), f32),
            pltpu.VMEM((4, 2, P_SIZE + 8, P_SIZE), f32),
            pltpu.VMEM((2, slice_rows, P_SIZE), bf16),
            pltpu.VMEM((2, P_SIZE, P_SIZE), f32),
            dma((5,)),
            dma,
            dma((3, 2, CHUNKS)),
            dma((8, CHUNKS)),
            dma((4, CHUNKS)),
            dma((W_PARTS,)),
            dma((W_PARTS,)),
            dma((W_PARTS,)),
            dma((W_PARTS,)),
            dma((2, W_PARTS)),
            dma((2, W_PARTS)),
            dma,
            dma,
            dma((2,)),
            dma((4,)),
            dma((4,)),
            dma((4,)),
            dma((4, CHUNKS)),
            dma((4, CHUNKS)),
            dma((4,)),
            dma((4,)),
            dma((2,)),
            dma((2,)),
            dma((2,)),
            dma((2,)),
            dma((2,)),
        ],
        compiler_params=pltpu.CompilerParams(
            collective_id=0, has_side_effects=True, vmem_limit_bytes=58 * 1024 * 1024
        ),
    )(
        span_id.T,
        prompt_adapter,
        owner_pos,
        slice_len.T,
        tokens,
        proj_weight,
        jnp.swapaxes(pool_down, 1, 2),
        pool_up,
        decay_rate.reshape(1, -1),
        norm_gain.reshape(1, -1),
    )


def solution(mesh):
    n, n_seq = mesh.shape["head"], mesh.shape["seq"]

    def body(
        tokens,
        proj_weight,
        decay_rate,
        norm_gain,
        pool_down,
        pool_up,
        span_id,
        prompt_adapter,
        owner_pos,
        slice_len,
    ):
        if n == 8 and n_seq == 4 and span_id.shape[1] == 2:
            return paired_call(
                (
                    tokens,
                    proj_weight,
                    decay_rate,
                    norm_gain,
                    pool_down,
                    pool_up,
                    span_id,
                    prompt_adapter,
                    owner_pos,
                    slice_len,
                )
            )
        rows, shard = tokens.shape
        model = proj_weight.shape[1]
        lanes = span_id.shape[1]
        per_owner, _, rank = pool_down.shape
        slice_rows = rows // lanes
        width = lanes * rank
        smem = pl.BlockSpec(memory_space=pltpu.SMEM)
        vmem = pl.BlockSpec(memory_space=pltpu.VMEM)
        hbm = pl.BlockSpec(memory_space=pl.ANY)
        dma = pltpu.SemaphoreType.DMA
        return pl.pallas_call(
            functools.partial(ring_kernel, n, n_seq),
            out_shape=(
                jax.ShapeDtypeStruct((rows, P_SIZE), jnp.bfloat16),
                jax.ShapeDtypeStruct((1, lanes, P_SIZE, P_SIZE), jnp.float32),
            ),
            in_specs=[smem, smem, smem, smem, vmem, hbm, hbm, vmem, vmem, vmem],
            out_specs=(vmem, vmem),
            scratch_shapes=[
                pltpu.VMEM((2, n // 2, rows, shard), jnp.bfloat16),
                pltpu.VMEM((model, 4 * P_SIZE), jnp.bfloat16),
                pltpu.VMEM((per_owner, model, rank), jnp.bfloat16),
                pltpu.VMEM((per_owner, rank, model), jnp.bfloat16),
                pltpu.VMEM((rows, 4 * P_SIZE), jnp.float32),
                pltpu.VMEM((per_owner, rows, rank), jnp.float32),
                pltpu.VMEM((n, width, P_SIZE), jnp.bfloat16),
                pltpu.VMEM((n, width, P_SIZE), jnp.bfloat16),
                pltpu.VMEM((slice_rows, width), jnp.bfloat16),
                pltpu.VMEM((n, slice_rows // n, width), jnp.bfloat16),
                pltpu.VMEM((n, slice_rows // n, width), jnp.bfloat16),
                pltpu.VMEM((lanes, P_SIZE + 8, P_SIZE), jnp.float32),
                pltpu.VMEM((n_seq, lanes, P_SIZE + 8, P_SIZE), jnp.float32),
                dma((5,)),
                dma((2, n // 2, PIECES)),
                dma((2, n // 2, PIECES)),
                dma((n,)),
                dma((n,)),
                dma((n,)),
                dma((n,)),
                dma((n,)),
                dma((n,)),
                dma((n_seq,)),
                dma((n_seq,)),
            ],
            compiler_params=pltpu.CompilerParams(
                collective_id=0, has_side_effects=True, vmem_limit_bytes=58 * 1024 * 1024
            ),
        )(
            span_id.T,
            prompt_adapter,
            owner_pos,
            slice_len.T,
            tokens,
            proj_weight,
            jnp.swapaxes(pool_down, 1, 2),
            pool_up,
            decay_rate.reshape(1, -1),
            norm_gain.reshape(1, -1),
        )

    in_specs = (
        P("seq", "head"),
        P(None, None, "head"),
        P("head"),
        P("head"),
        P("head", None, None),
        P("head", None, None),
        P(),
        P(),
        P(),
        P(),
    )
    out_specs = (P("seq", "head"), P("seq", None, "head", None))
    return jax.shard_map(body, mesh=mesh, in_specs=in_specs, out_specs=out_specs, check_vma=False)
```

```python
import functools
import math

import jax
import jax.numpy as jnp
from jax import lax
from jax.experimental import pallas as pl
from jax.experimental.pallas import tpu as pltpu
from jax.sharding import PartitionSpec as P

P_SIZE = 128
NORM_FLOOR = 1.0
PIECES = 4
CHUNKS = 4
W_PARTS = 8
LATE = 3
MESH = pl.DeviceIdType.MESH
HIGHEST = lax.Precision.HIGHEST


def grid_of(n):
    across = math.isqrt(n // 2)
    if across >= 2 and 2 * across * across == n:
        return across, n // across
    return 1, n


def head_at(position, n):
    across, depth = grid_of(n)
    if across == 1:
        return position
    width = across - 1
    back = lax.div(lax.div(position, depth) + (across - 1), across)
    rest = (position - depth) * back
    row, step = lax.div(rest, width), lax.rem(rest, width)
    x = 1 + step + lax.rem(row, 2) * (width - 1 - 2 * step)
    return (1 - back) * position * across + back * ((depth - 1 - row) * across + x)


def position_of(head, n):
    across, depth = grid_of(n)
    if across == 1:
        return head
    width = across - 1
    z, x = lax.div(head, across), lax.rem(head, across)
    back = lax.div(x + across - 1, across)
    row, step = depth - 1 - z, (x - 1) * back
    moved = step + lax.rem(row, 2) * (width - 1 - 2 * step)
    return (1 - back) * z + back * (depth + row * width + moved)


def dot(a, b, precision=None):
    return jnp.dot(a, b, preferred_element_type=jnp.float32, precision=precision)


def ring_kernel(
    n,
    n_seq,
    span_ref,
    prompt_ref,
    owner_ref,
    len_ref,
    tok_ref,
    w_hbm,
    down_hbm,
    up_ref,
    rate_ref,
    gain_ref,
    out_ref,
    state_ref,
    slots,
    wbuf,
    dbuf,
    dturn,
    acc,
    lacc,
    up_send,
    up_recv,
    low_send,
    low_recv,
    low_full,
    st_send,
    st_recv,
    w_sem,
    ring_send,
    ring_recv,
    up_ssem,
    up_rsem,
    rs_ssem,
    rs_rsem,
    ag_ssem,
    ag_rsem,
    st_ssem,
    st_rsem,
):
    me = lax.axis_index("head")
    seq = lax.axis_index("seq")
    rows, shard = tok_ref.shape
    lanes = span_ref.shape[0]
    per_owner = down_hbm.shape[0]
    rank = down_hbm.shape[1]
    slice_rows = rows // lanes
    piece = rows // PIECES
    half = n // 2
    here = position_of(me, n)
    right = head_at(lax.rem(here + 1, n), n)
    left = head_at(lax.rem(here + n - 1, n), n)
    toward = (right, left)

    loads = [
        pltpu.make_async_copy(w_hbm.at[c], wbuf.at[:, pl.ds(c * P_SIZE, P_SIZE)], w_sem.at[c])
        for c in range(4)
    ]
    loads.append(pltpu.make_async_copy(down_hbm, dturn, w_sem.at[4]))

    barrier = pltpu.get_barrier_semaphore()

    def greet_head(d, carry):
        pl.semaphore_signal(
            barrier, inc=1, device_id={"head": lax.rem(me + d, n)}, device_id_type=MESH
        )
        return carry

    def greet_seq(d, carry):
        pl.semaphore_signal(
            barrier, inc=1, device_id={"seq": lax.rem(seq + d, n_seq)}, device_id_type=MESH
        )
        return carry

    lax.fori_loop(1, n, greet_head, 0)
    lax.fori_loop(1, n_seq, greet_seq, 0)
    for load in loads:
        load.start()
    pl.semaphore_wait(barrier, n - 1 + n_seq - 1)

    def hop(direction, step, p, own=False):
        span = pl.ds(p * piece, piece)
        source = tok_ref.at[span] if own else slots.at[direction, step - 2, span]
        return pltpu.make_async_remote_copy(
            src_ref=source,
            dst_ref=slots.at[direction, step - 1, span],
            send_sem=ring_send.at[direction, step - 1, p],
            recv_sem=ring_recv.at[direction, step - 1, p],
            device_id={"head": toward[direction]},
            device_id_type=MESH,
        )

    def long_way(direction, p):
        return p % 2 == direction

    for k in range(PIECES):
        for direction in range(2):
            hop(direction, 1, (k + direction) % PIECES, own=True).start()

    places = [owner_ref[prompt_ref[span_ref[j, seq]]] for j in range(lanes)]
    owned = [
        [jnp.where(places[j] == me * per_owner + s, 1.0, 0.0).astype(jnp.float32) for s in range(per_owner)]
        for j in range(lanes)
    ]

    for j in range(lanes):
        mine = sum(owned[j][s] * up_ref[s].astype(jnp.float32) for s in range(per_owner)).astype(jnp.bfloat16)
        for i in range(n):
            up_send[i, pl.ds(j * rank, rank), :] = mine[:, i * P_SIZE : (i + 1) * P_SIZE]

    def up_copy(d):
        peer = lax.rem(me + d, n)
        return pltpu.make_async_remote_copy(
            src_ref=up_send.at[peer],
            dst_ref=up_recv.at[d],
            send_sem=up_ssem.at[d],
            recv_sem=up_rsem.at[d],
            device_id={"head": peer},
            device_id_type=MESH,
        )

    def up_start(d, carry):
        up_copy(d).start()
        return carry

    lax.fori_loop(1, n, up_start, 0)
    up_recv[0] = up_send[me]

    for load in loads:
        load.wait()

    strip = wbuf.shape[0] // 12

    def turn_strip(i, carry):
        deep = pl.ds(pl.multiple_of(i * strip, strip), strip)
        for s in range(per_owner):
            dbuf[s, deep, :] = dturn[s, :, deep].T
        return carry

    lax.fori_loop(0, 12, turn_strip, 0)

    def multiply(x, span, origin, first=False):
        deep = pl.ds(pl.multiple_of(origin * shard, 64), shard)
        gained = dot(x, wbuf[deep, :])
        lows = [dot(x, dbuf[s, deep, :]) for s in range(per_owner)]
        if first:
            acc[span, :] = gained
            for s in range(per_owner):
                lacc[s, span, :] = lows[s]
        else:
            acc[span, :] += gained
            for s in range(per_owner):
                lacc[s, span, :] += lows[s]

    def own_piece(p, carry):
        span = pl.ds(pl.multiple_of(p * piece, piece), piece)
        multiply(tok_ref[span, :], span, me, first=True)
        return carry

    lax.fori_loop(0, PIECES, own_piece, 0)

    def arrive(step, forward, present):
        order = [((k + d) % PIECES, d) for k in range(PIECES) for d in range(2)]
        order = [(p, d) for p, d in order if present(d, p)]
        for p, d in order:
            hop(d, step, p).wait_recv() if not isinstance(step, int) or step > 1 else hop(d, 1, p, own=True).wait_recv()
            if forward(d, p):
                hop(d, step + 1, p).start()
            sign = n - step if d == 0 else step
            origin = head_at(lax.rem(here + sign, n), n)
            span = pl.ds(p * piece, piece)
            multiply(slots[d, step - 1, span, :], span, origin)

    everything = lambda d, p: True
    nothing = lambda d, p: False
    if half >= 2:
        arrive(1, everything if half > 2 else long_way, everything)
    if half > 3:

        def middle(step, carry):
            arrive(step, everything, everything)
            return carry

        lax.fori_loop(2, half - 1, middle, 0)
    if half > 2:
        arrive(half - 1, long_way, everything)
    arrive(half, nothing, long_way)

    width = lanes * rank
    for j in range(lanes):
        span = pl.ds(j * slice_rows, slice_rows)
        mine = sum(owned[j][s] * lacc[s, span, :] for s in range(per_owner)).astype(jnp.bfloat16)
        low_send[:, pl.ds(j * rank, rank)] = mine
    block = slice_rows // n

    def rs_copy(d):
        peer = lax.rem(me + d, n)
        return pltpu.make_async_remote_copy(
            src_ref=low_send.at[pl.ds(pl.multiple_of(peer * block, block), block)],
            dst_ref=low_recv.at[d],
            send_sem=rs_ssem.at[d],
            recv_sem=rs_rsem.at[d],
            device_id={"head": peer},
            device_id_type=MESH,
        )

    def ag_copy(d):
        peer = lax.rem(me + d, n)
        return pltpu.make_async_remote_copy(
            src_ref=low_recv.at[0],
            dst_ref=low_full.at[me],
            send_sem=ag_ssem.at[d],
            recv_sem=ag_rsem.at[d],
            device_id={"head": peer},
            device_id_type=MESH,
        )

    def ag_arrival(d):
        peer = lax.rem(me + n - d, n)
        return pltpu.make_async_remote_copy(
            src_ref=low_recv.at[0],
            dst_ref=low_full.at[peer],
            send_sem=ag_ssem.at[d],
            recv_sem=ag_rsem.at[d],
            device_id={"head": peer},
            device_id_type=MESH,
        )

    def each(count, act):
        def turn(d, carry):
            act(d)
            return carry

        lax.fori_loop(1, count, turn, 0)

    each(n, lambda d: rs_copy(d).start())
    each(n, lambda d: up_copy(d).wait_recv())
    up = jnp.sum(up_recv[...].astype(jnp.float32), axis=0).astype(jnp.bfloat16)
    total = low_send[pl.ds(pl.multiple_of(me * block, block), block), :].astype(jnp.float32)
    each(n, lambda d: rs_copy(d).wait_recv())
    for d in range(1, n):
        total = total + low_recv[d].astype(jnp.float32)
    low_recv[0] = total.astype(jnp.bfloat16)
    each(n, lambda d: ag_copy(d).start())
    low_full[me] = total.astype(jnp.bfloat16)

    slot_ids = lax.broadcasted_iota(jnp.int32, (slice_rows, 1), 0)
    causal = lax.broadcasted_iota(jnp.int32, (slice_rows, slice_rows), 0) >= lax.broadcasted_iota(
        jnp.int32, (slice_rows, slice_rows), 1
    )
    triangle = jnp.where(causal, 1.0, 0.0).astype(jnp.float32)
    columns = lax.broadcasted_iota(jnp.int32, (1, width), 1)
    each(n, lambda d: ag_arrival(d).wait_recv())
    low = low_full[...].reshape(slice_rows, width).astype(jnp.float32)

    kept = []
    for j in range(lanes):
        span = pl.ds(j * slice_rows, slice_rows)
        own = (columns >= j * rank) & (columns < (j + 1) * rank)
        gate = acc[span, pl.ds(3 * P_SIZE, P_SIZE)] + dot(jnp.where(own, low, 0.0).astype(jnp.bfloat16), up)
        live = jnp.where(slot_ids < len_ref[j, seq], 1.0, 0.0).astype(jnp.float32)
        step_log = -(live * rate_ref[...] * (2.0 * jax.nn.sigmoid(gate)))
        cumul = dot(triangle, step_log, HIGHEST)
        query = acc[span, pl.ds(0, P_SIZE)].astype(jnp.bfloat16).astype(jnp.float32)
        key = acc[span, pl.ds(P_SIZE, P_SIZE)].astype(jnp.bfloat16).astype(jnp.float32) * (
            live * P_SIZE ** (-0.5)
        )
        value = acc[span, pl.ds(2 * P_SIZE, P_SIZE)].astype(jnp.bfloat16).astype(jnp.float32)
        last = cumul[slice_rows - 1 :, :]
        carried = lax.dot_general(
            key * jnp.exp(last - cumul),
            value,
            (((0,), (0,)), ((), ())),
            precision=HIGHEST,
            preferred_element_type=jnp.float32,
        )
        st_send[j, pl.ds(0, P_SIZE), :] = carried
        st_send[j, pl.ds(P_SIZE, 8), :] = jnp.broadcast_to(jnp.exp(last), (8, P_SIZE))
        kept.append((live, query * jnp.exp(cumul), key * jnp.exp(-cumul), value))

    def st_copy(d):
        return pltpu.make_async_remote_copy(
            src_ref=st_send,
            dst_ref=st_recv.at[seq],
            send_sem=st_ssem.at[d],
            recv_sem=st_rsem.at[d],
            device_id={"seq": lax.rem(seq + d, n_seq)},
            device_id_type=MESH,
        )

    def st_arrival(d):
        peer = lax.rem(seq + n_seq - d, n_seq)
        return pltpu.make_async_remote_copy(
            src_ref=st_send,
            dst_ref=st_recv.at[peer],
            send_sem=st_ssem.at[d],
            recv_sem=st_rsem.at[d],
            device_id={"seq": peer},
            device_id_type=MESH,
        )

    each(n_seq, lambda d: st_copy(d).start())
    st_recv[seq] = st_send[...]

    inners = []
    for j in range(lanes):
        live, query_decay, key_decay, value = kept[j]
        scores = lax.dot_general(
            query_decay,
            key_decay,
            (((1,), (1,)), ((), ())),
            precision=HIGHEST,
            preferred_element_type=jnp.float32,
        )
        inners.append(dot(jnp.where(causal, scores, 0.0), value, HIGHEST))

    each(n_seq, lambda d: st_arrival(d).wait_recv())
    for j in range(lanes):
        live, query_decay, _, _ = kept[j]
        span = pl.ds(j * slice_rows, slice_rows)
        ended = jnp.zeros((P_SIZE, P_SIZE), jnp.float32)
        start = ended
        final = ended
        for k in range(n_seq):
            if k:
                same = jnp.where(span_ref[j, k] == span_ref[j, k - 1], 1.0, 0.0).astype(jnp.float32)
                begun = same * ended
            else:
                begun = ended
            decay = jnp.broadcast_to(st_recv[k, j, pl.ds(P_SIZE, 1), :], (P_SIZE, P_SIZE)).T
            ended = decay * begun + st_recv[k, j, pl.ds(0, P_SIZE), :]
            at = jnp.where(seq == k, 1.0, 0.0).astype(jnp.float32)
            start = start + at * begun
            final = final + at * ended
        inner = inners[j] + dot(query_decay, start, HIGHEST)
        scale = lax.rsqrt(jnp.maximum(jnp.mean(inner * inner, axis=-1, keepdims=True), NORM_FLOOR))
        out_ref[span, :] = (inner * scale * gain_ref[...] * live).astype(jnp.bfloat16)
        state_ref[0, j] = final

    each(n, lambda d: up_copy(d).wait_send())
    each(n, lambda d: rs_copy(d).wait_send())
    each(n, lambda d: ag_copy(d).wait_send())
    each(n_seq, lambda d: st_copy(d).wait_send())
    for p in range(PIECES):
        for direction in range(2):
            hop(direction, 1, p, own=True).wait_send()
    for direction in range(2):
        for p in range(PIECES):
            reach = half if long_way(direction, p) else half - 1

            def drained(step, carry):
                hop(direction, step, p).wait_send()
                return carry

            lax.fori_loop(2, reach + 1, drained, 0)


def halves(a):
    high = a.astype(jnp.bfloat16)
    return high, (a - high.astype(jnp.float32)).astype(jnp.bfloat16)


def across_rows(a, b):
    return lax.dot_general(a, b, (((1,), (1,)), ((), ())), preferred_element_type=jnp.float32)


def down_rows(a, b):
    return lax.dot_general(a, b, (((0,), (0,)), ((), ())), preferred_element_type=jnp.float32)


def paired_kernel(
    span_ref,
    prompt_ref,
    owner_ref,
    len_ref,
    tok_ref,
    w_hbm,
    down_hbm,
    up_ref,
    rate_ref,
    gain_ref,
    out_ref,
    state_ref,
    tokbuf,
    wbuf,
    dturn,
    dsend,
    din,
    dbuf,
    acc,
    lacc,
    lowb,
    upsend,
    upin,
    upsum,
    upr,
    rgbuf,
    qdh,
    qdl,
    inn,
    run,
    carry,
    st_send,
    st_recv,
    obuf,
    fbuf,
    w_sem,
    t_local,
    t_send,
    t_recv,
    f_send,
    wz_send,
    wz_recv,
    wy_send,
    wy_recv,
    wc_send,
    wc_recv,
    r_send,
    r_recv,
    p_send,
    p_recv,
    u_send,
    u_recv,
    l_send,
    l_recv,
    s_send,
    s_recv,
    o_send,
    o_recv,
    e_send,
    e_recv,
    o_local,
):
    h = lax.axis_index("head")
    s = lax.axis_index("seq")
    z, x = lax.div(h, 2), lax.rem(h, 2)
    y, k = lax.div(s, 2), lax.rem(s, 2)
    b, p = lax.div(z, 2), lax.rem(z, 2)
    zi, z2, z3 = z + 1 - 2 * p, lax.rem(z + 2, 4), 3 - z
    same = k == p
    differ = k != p
    inner = (z == 1) | (z == 2)
    outer = (z == 0) | (z == 3)
    inward = 1 + p
    seqc = 2 * y + p
    lane = k

    rows, shard = tok_ref.shape
    lanes = span_ref.shape[0]
    per_owner, rank, model = down_hbm.shape
    slice_rows = rows // lanes
    chunk = slice_rows // CHUNKS
    deep_part = model // W_PARTS
    wide = 4 * P_SIZE

    def at(xx, yy, zz, kk):
        return {"head": 2 * zz + xx, "seq": 2 * yy + kk}

    def remote(src, dst, send, recv, where):
        return pltpu.make_async_remote_copy(
            src_ref=src, dst_ref=dst, send_sem=send, recv_sem=recv, device_id=where, device_id_type=MESH
        )

    loads = [
        pltpu.make_async_copy(
            w_hbm.at[c],
            wbuf.at[:, pl.ds(pl.multiple_of(p * wide + c * P_SIZE, P_SIZE), P_SIZE)],
            w_sem.at[c],
        )
        for c in range(4)
    ]
    pools = pltpu.make_async_copy(down_hbm, dturn, w_sem.at[4])

    barrier = pltpu.get_barrier_semaphore()
    plane = 2 * h + k

    def greet(d, c):
        other = lax.rem(plane + d, 16)
        where = {"head": lax.div(other, 2), "seq": 2 * y + lax.rem(other, 2)}
        pl.semaphore_signal(barrier, inc=1, device_id=where, device_id_type=MESH)
        return c

    lax.fori_loop(1, 16, greet, 0)
    for zz in (z, zi):
        pl.semaphore_signal(barrier, inc=1, device_id=at(x, 1 - y, zz, k), device_id_type=MESH)
    pools.start()
    rgbuf[p, pl.ds(0, 1), :] = rate_ref[...]
    rgbuf[p, pl.ds(1, 1), :] = gain_ref[...]
    pl.semaphore_wait(barrier, 17)

    def deep_at(i):
        return pl.ds(pl.multiple_of(i * deep_part, 128), deep_part)

    def col_at(q, c):
        return pl.ds(pl.multiple_of(q * wide + c * P_SIZE, P_SIZE), P_SIZE)

    def wz_copy(i):
        c = 2 * y + k
        return remote(
            w_hbm.at[c, deep_at(i)],
            wbuf.at[deep_at(i), col_at(p, c)],
            wz_send.at[i],
            wz_recv.at[i],
            at(x, y, zi, k),
        )

    def held(i, c):
        return wbuf.at[deep_at(i), col_at(1 - p, c)]

    def wz_arrival(i):
        c = 2 * y + k
        return remote(held(i, c), held(i, c), wz_send.at[i], wz_recv.at[i], at(x, y, zi, k))

    def wy_copy(i):
        c = 2 * y + k
        return remote(held(i, c), held(i, c), wy_send.at[i], wy_recv.at[i], at(x, 1 - y, z, k))

    def wy_arrival(i):
        c = 2 * (1 - y) + k
        return remote(held(i, c), held(i, c), wy_send.at[i], wy_recv.at[i], at(x, 1 - y, z, k))

    def wc_copy(g, i):
        c = 2 * (y + g - 2 * y * g) + k
        return remote(held(i, c), held(i, c), wc_send.at[g, i], wc_recv.at[g, i], at(x, y, z, 1 - k))

    def wc_arrival(g, i):
        c = 2 * (y + g - 2 * y * g) + 1 - k
        return remote(held(i, c), held(i, c), wc_send.at[g, i], wc_recv.at[g, i], at(x, y, z, 1 - k))

    def each(first, count, act):
        def turn(i, c):
            act(i)
            return c

        lax.fori_loop(first, count, turn, 0)

    each(0, 2, lambda i: wz_copy(i).start())

    def mask(seq):
        spot = owner_ref[prompt_ref[span_ref[lane, seq]]]
        return [jnp.where(spot == h * per_owner + i, 1.0, 0.0).astype(jnp.float32) for i in range(per_owner)]

    mine, theirs = mask(seqc), mask(2 * y + 1 - p)
    for g in range(4):
        for q in range(2):
            head = 4 * (g // 2) + 2 * q + g % 2
            part = [up_ref[o, :, head * P_SIZE : (head + 1) * P_SIZE].astype(jnp.float32) for o in range(per_owner)]
            upsend[g, q] = sum(theirs[o] * part[o] for o in range(per_owner)).astype(jnp.bfloat16)
            upsum[g, q] = sum(mine[o] * part[o] for o in range(per_owner)).astype(jnp.bfloat16)

    from_outer = jnp.where(inner, 1, 0)
    pan_copy = remote(dsend, din.at[from_outer], p_send.at[0], p_recv.at[from_outer], at(x, y, inward, k))
    upp_copy = remote(upsend, upin.at[from_outer], p_send.at[1], p_recv.at[2 + from_outer], at(x, y, inward, k))
    upp_copy.start()
    each(2, W_PARTS, lambda i: wz_copy(i).start())
    for load in loads:
        load.start()

    rg_copy = remote(rgbuf.at[p], rgbuf.at[p], r_send, r_recv, at(x, y, zi, k))
    rg_arrival = remote(rgbuf.at[1 - p], rgbuf.at[1 - p], r_send, r_recv, at(x, y, zi, k))
    rg_copy.start()

    def chunk_at(r):
        return pl.ds(pl.multiple_of(r * chunk, chunk), chunk)

    def place(f, r):
        return tokbuf.at[chunk_at(r), pl.ds(pl.multiple_of(f * shard, 128), shard)]

    def tok_copy(t, j, r, where):
        source = tok_ref.at[pl.ds(pl.multiple_of(j * slice_rows + r * chunk, chunk), chunk)]
        return remote(source, place(h, r), t_send.at[t, j, r], t_recv.at[h, r], where)

    def free_sends(r, act):
        @pl.when(same)
        def _():
            act(tok_copy(0, 1 - k, r, at(x, y, z, 1 - k)))
            for j in range(2):
                act(tok_copy(1, j, r, at(1 - x, y, z, j)))

        @pl.when(differ & inner)
        def _():
            for j in range(2):
                act(tok_copy(2, j, r, at(x, y, z3, j)))

    def late_sends(r, act):
        @pl.when(same)
        def _():
            for j in range(2):
                act(tok_copy(2, j, r, at(x, y, z2, j)))

        @pl.when(differ)
        def _():
            for j in range(2):
                act(tok_copy(1, j, r, at(x, y, zi, j)))

    own = pltpu.make_async_copy(
        tok_ref.at[pl.ds(pl.multiple_of(lane * slice_rows, chunk), slice_rows)],
        tokbuf.at[:, pl.ds(pl.multiple_of(h * shard, 128), shard)],
        t_local,
    )

    each(0, CHUNKS, lambda r: free_sends(r, lambda copy: copy.start()))

    @pl.when(same)
    def _():
        own.start()

    pools.wait()
    half_model = model // 2
    strips = 6
    strip = half_model // strips

    def strip_at(i, base=0):
        return pl.ds(pl.multiple_of(base + i * strip, 128), strip)

    def pick(weights, i):
        both = [
            sum(weights[o] * dturn[o, :, strip_at(i, base)].astype(jnp.float32) for o in range(per_owner))
            for base in (0, half_model)
        ]
        return jnp.concatenate(both, axis=0).astype(jnp.bfloat16).T

    def fill(i):
        dsend[strip_at(i), :] = pick(theirs, i)
        dbuf[strip_at(i), :] = pick(mine, i)

    each(0, strips, fill)

    def arrived(f, r):
        remote(place(f, r), place(f, r), t_send.at[0, 0, 0], t_recv.at[f, r], at(1 - x, y, z, k)).wait_recv()

    def x_forward(a, zz, r):
        f = 2 * zz + x
        return remote(place(f, r), place(f, r), f_send.at[a - 1, r], t_recv.at[f, r], at(1 - x, y, z, k))

    def z_forward(r):
        f = 2 * zi + x
        return remote(place(f, r), place(f, r), f_send.at[3, r], t_recv.at[f, r], at(x, y, z2, k))

    @pl.when(inner)
    def _():
        pan_copy.start()

    mates = [None, at(1 - x, y, z, k), at(x, y, z2, k), at(1 - x, y, z2, k)]
    groups = [2 * b + x, 2 * b + 1 - x, 2 * (1 - b) + x, 2 * (1 - b) + 1 - x]

    def up_copy(d):
        return remote(upsum.at[groups[d]], upr.at[d], u_send.at[d], u_recv.at[d], mates[d])

    @pl.when(outer)
    def _():
        for d in range(1, 4):
            up_copy(d).start()

    def spread(i, c):
        wz_arrival(i).wait_recv()
        wy_copy(i).start()
        wc_copy(0, i).start()

        @pl.when(i > 0)
        def _():
            wy_arrival(i - 1).wait_recv()
            wc_copy(1, i - 1).start()

        @pl.when(inner & (lax.rem(i, W_PARTS // CHUNKS) == 0))
        def _():
            r = lax.div(i, W_PARTS // CHUNKS)
            arrived(2 * z3 + x, r)
            x_forward(3, z3, r).start()

        @pl.when(inner & (i == 4))
        def _():
            whole = upsum[...].astype(jnp.float32)
            for g in range(2):
                remote(upsend, upin.at[g], p_send.at[1], p_recv.at[2 + g], at(x, y, zi, k)).wait_recv()
                whole = whole + upin[g].astype(jnp.float32)
            upsum[...] = whole.astype(jnp.bfloat16)
            for d in range(1, 4):
                up_copy(d).start()

        @pl.when((i == LATE) & outer)
        def _():
            pan_copy.start()

        @pl.when(i == LATE)
        def _():
            each(0, CHUNKS, lambda r: late_sends(r, lambda copy: copy.start()))

        @pl.when(outer & (i >= W_PARTS - CHUNKS))
        def _():
            r = i - (W_PARTS - CHUNKS)
            arrived(2 * z2 + x, r)
            x_forward(2, z2, r).start()

        return c

    lax.fori_loop(0, W_PARTS, spread, 0)
    wy_arrival(W_PARTS - 1).wait_recv()
    wc_copy(1, W_PARTS - 1).start()

    def gather_down():
        @pl.when(inner)
        def _():
            for g in range(2):
                remote(dsend, din.at[g], p_send.at[0], p_recv.at[g], at(x, y, zi, k)).wait_recv()

            def turn(i):
                whole = dbuf[strip_at(i), :].astype(jnp.float32)
                for g in range(2):
                    whole = whole + din[g, strip_at(i), :].astype(jnp.float32)
                dbuf[strip_at(i), :] = whole.astype(jnp.bfloat16)

            each(0, strips, turn)

    upr[0] = upsum[groups[0]]

    def packed_at(r):
        return pl.ds(pl.multiple_of(r * (chunk // 2), chunk // 2), chunk // 2)

    def low_copy(d, r):
        span = packed_at(r)
        return remote(lowb.at[0, span], lowb.at[d, span], l_send.at[d, r], l_recv.at[d, r], mates[d])

    run[...] = jnp.zeros_like(run)
    carry[...] = jnp.zeros_like(carry)

    def shard_of(a, column):
        high, bit = lax.div(a, 2), lax.rem(a, 2)
        zz = 2 * (b + high - 2 * b * high) + p + bit - 2 * p * bit
        return 2 * zz + column

    low_half = lax.div(lax.broadcasted_iota(jnp.int32, (1, P_SIZE), 1), rank)

    def multiply(f, r, first):
        span = chunk_at(r)
        deep = pl.ds(pl.multiple_of(f * shard, 128), shard)
        block = tokbuf[span, deep]
        late = lax.div(f, 4)
        packed = pl.ds(pl.multiple_of((f - 4 * late) * shard, 128), shard)
        low_part = jnp.where(low_half == late, dot(block, dbuf[packed, :]), 0.0)
        part = dot(block, wbuf[deep, :])

        @pl.when(first)
        def _():
            lacc[...] = low_part
            acc[span, :] = part

        @pl.when(jnp.logical_not(first))
        def _():
            lacc[...] += low_part
            acc[span, :] += part

    def onward(a, zz, r):
        arrived(2 * zz + x, r)
        x_forward(a, zz, r).start()

    def advance(r):
        @pl.when(inner)
        def _():
            onward(1, zi, r)
            z_forward(r).start()
            onward(2, z2, r)

        @pl.when(outer)
        def _():
            onward(3, z3, r)

            @pl.when(r + 2 < CHUNKS)
            def _():
                onward(1, zi, r + 2)

        @pl.when(differ)
        def _():
            arrived(h, r)

        @pl.when(same & (r == 0))
        def _():
            own.wait()

    soon = jnp.where(inner, 3, 2)

    def other(a, r):
        f = shard_of(a, 1 - x)
        arrived(f, r)
        multiply(f, r, a < 0)

    def early(r):
        each(0, 4, lambda a: multiply(shard_of(a, x), r, a == 0))
        each(0, 2, lambda i: other(i * soon, r))

    def finish(r):
        second, step_to = jnp.where(inner, 2, 1), jnp.where(inner, -1, 2)
        each(0, 2, lambda i: other(second + i * step_to, r))
        low_sum = (lacc[:, :rank] + lacc[:, rank:]).astype(jnp.bfloat16)
        lowb[0, packed_at(r), :] = jnp.concatenate([low_sum[: chunk // 2], low_sum[chunk // 2 :]], axis=1)
        for d in range(1, 4):
            low_copy(d, r).start()

    row_ids = lax.broadcasted_iota(jnp.int32, (chunk, chunk), 0)
    column_ids = lax.broadcasted_iota(jnp.int32, (chunk, chunk), 1)
    causal = row_ids >= column_ids
    triangle = jnp.where(causal, 1.0, 0.0).astype(jnp.bfloat16)
    slot_ids = lax.broadcasted_iota(jnp.int32, (slice_rows, 1), 0)
    chunk_ids = lax.broadcasted_iota(jnp.int32, (chunk, 1), 0)
    length = len_ref[lane, seqc]

    def state_copy(d):
        where = [None, at(x, 1 - y, z, k), at(x, y, zi, k), at(x, 1 - y, zi, k)][d]
        return remote(st_send, st_recv.at[seqc], s_send.at[d], s_recv.at[d], where)

    def state_arrival(d):
        yy, pp = [None, (1 - y, p), (y, 1 - p), (1 - y, 1 - p)][d]
        return remote(st_send, st_recv.at[2 * yy + pp], s_send.at[d], s_recv.at[d], at(x, 1 - y, z, k))

    def attend(r):
        span = chunk_at(r)

        @pl.when(r == 0)
        def _():
            for d in range(1, 4):
                up_copy(d).wait_recv()
            for q in range(2):
                upr[0, q] = sum(upr[d, q].astype(jnp.float32) for d in range(4)).astype(jnp.bfloat16)

        for d in range(1, 4):
            low_copy(d, r).wait_recv()
        low = sum(lowb[d, packed_at(r), :].astype(jnp.float32) for d in range(4)).astype(jnp.bfloat16)
        low = jnp.concatenate([low[:, :rank], low[:, rank:]], axis=0)
        live = jnp.where(chunk_ids + r * chunk < length, 1.0, 0.0).astype(jnp.float32)
        kept = []
        for q in range(2):
            first = q * wide
            gate = acc[span, first + 3 * P_SIZE : first + 4 * P_SIZE] + dot(low, upr[0, q])
            step_log = -(live * rgbuf[q, pl.ds(0, 1), :] * (2.0 * jax.nn.sigmoid(gate)))
            a0, rest = halves(step_log)[0], step_log
            rest = rest - a0.astype(jnp.float32)
            a1, a2 = halves(rest)
            cumul = dot(triangle, a0) + (dot(triangle, a1) + dot(triangle, a2)) + carry[q, pl.ds(0, 1), :]
            carry[q] = jnp.broadcast_to(cumul[chunk - 1 :, :], (8, P_SIZE))
            query = acc[span, first : first + P_SIZE].astype(jnp.bfloat16).astype(jnp.float32)
            key = acc[span, first + P_SIZE : first + 2 * P_SIZE].astype(jnp.bfloat16).astype(jnp.float32) * (
                live * P_SIZE ** (-0.5)
            )
            value = acc[span, first + 2 * P_SIZE : first + 3 * P_SIZE].astype(jnp.bfloat16)
            q_high, q_low = halves(query * jnp.exp(cumul))
            k_high, k_low = halves(key * jnp.exp(-cumul))
            qdh[q, span, :] = q_high
            qdl[q, span, :] = q_low
            before = run[q]
            run[q] = before + (down_rows(k_high, value) + down_rows(k_low, value))
            kept.append((q_high, q_low, k_high, k_low, value, before))

        @pl.when(r == CHUNKS - 1)
        def _():
            for q in range(2):
                st_send[q, pl.ds(0, P_SIZE), :] = run[q]
                st_send[q, pl.ds(P_SIZE, 8), :] = jnp.exp(carry[q])
            for d in range(1, 4):
                state_copy(d).start()
            st_recv[seqc] = st_send[...]

        for q in range(2):
            q_high, q_low, k_high, k_low, value, before = kept[q]
            scores = across_rows(q_high, k_high) + (across_rows(q_high, k_low) + across_rows(q_low, k_high))
            s_high, s_low = halves(jnp.where(causal, scores, 0.0))
            b_high, b_low = halves(before)
            inn[q, span, :] = (
                dot(s_high, value)
                + dot(s_low, value)
                + dot(q_high, b_high)
                + (dot(q_high, b_low) + dot(q_low, b_high))
            )

    @pl.when(outer)
    def _():
        each(0, 2, lambda r: onward(1, zi, r))

    for i in range(4):
        loads[i].wait()
    each(0, W_PARTS, lambda i: wc_arrival(0, i).wait_recv())
    each(0, W_PARTS, lambda i: wc_arrival(1, i).wait_recv())
    rg_arrival.wait_recv()
    def step(t, c):
        @pl.when(t < CHUNKS)
        def _():
            advance(t)

        @pl.when(t == 0)
        def _():
            gather_down()

        @pl.when((t > 0) & (t <= CHUNKS))
        def _():
            finish(t - 1)

        @pl.when(t < CHUNKS)
        def _():
            early(t)

        @pl.when(t > 2)
        def _():
            attend(t - 3)

        return c

    lax.fori_loop(0, CHUNKS + 3, step, 0)

    for d in range(1, 4):
        state_arrival(d).wait_recv()
    alive = jnp.where(slot_ids < length, 1.0, 0.0).astype(jnp.float32)

    def out_copy(q, where):
        return remote(
            obuf.at[q],
            out_ref.at[pl.ds(pl.multiple_of(lane * slice_rows, chunk), slice_rows)],
            o_send.at[q],
            o_recv.at[lane],
            where,
        )

    def end_copy(q, where):
        return remote(fbuf.at[q], state_ref.at[0, lane], e_send.at[q], e_recv.at[lane], where)

    keep_out = pltpu.make_async_copy(
        obuf.at[p], out_ref.at[pl.ds(pl.multiple_of(lane * slice_rows, chunk), slice_rows)], o_local.at[0]
    )
    keep_end = pltpu.make_async_copy(fbuf.at[p], state_ref.at[0, lane], o_local.at[1])
    away, beside = at(x, y, zi, p), at(x, y, z, 1 - k)

    for i in range(2):
        q = 1 - p if i == 0 else p
        ended = jnp.zeros((P_SIZE, P_SIZE), jnp.float32)
        start = ended
        final = ended
        for g in range(4):
            if g:
                kin = jnp.where(span_ref[lane, g] == span_ref[lane, g - 1], 1.0, 0.0).astype(jnp.float32)
                begun = kin * ended
            else:
                begun = ended
            decay = jnp.broadcast_to(st_recv[g, q, pl.ds(P_SIZE, 1), :], (P_SIZE, P_SIZE)).T
            ended = decay * (begun + st_recv[g, q, pl.ds(0, P_SIZE), :])
            now = jnp.where(seqc == g, 1.0, 0.0).astype(jnp.float32)
            start = start + now * begun
            final = final + now * ended
        fbuf[q] = final
        b_high, b_low = halves(start)
        total = inn[q] + dot(qdh[q], b_high) + (dot(qdh[q], b_low) + dot(qdl[q], b_high))
        scale = lax.rsqrt(jnp.maximum(jnp.mean(total * total, axis=-1, keepdims=True), NORM_FLOOR))
        obuf[q] = (total * scale * rgbuf[q, pl.ds(1, 1), :] * alive).astype(jnp.bfloat16)
        if i == 0:
            end_copy(q, away).start()
            out_copy(q, away).start()
        else:

            @pl.when(same)
            def _():
                keep_end.start()
                keep_out.start()

            @pl.when(differ)
            def _():
                end_copy(p, beside).start()
                out_copy(p, beside).start()

    def landed(j):
        span = pl.ds(pl.multiple_of(j * slice_rows, chunk), slice_rows)
        remote(obuf.at[0], out_ref.at[span], o_send.at[0], o_recv.at[j], beside).wait_recv()
        remote(fbuf.at[0], state_ref.at[0, j], e_send.at[0], e_recv.at[j], beside).wait_recv()

    landed(1 - k)

    @pl.when(same)
    def _():
        keep_end.wait()
        keep_out.wait()

    @pl.when(differ)
    def _():
        landed(k)
        end_copy(p, beside).wait_send()
        out_copy(p, beside).wait_send()

    end_copy(1 - p, away).wait_send()
    out_copy(1 - p, away).wait_send()
    each(0, W_PARTS, lambda i: wz_copy(i).wait_send())
    each(0, W_PARTS, lambda i: wy_copy(i).wait_send())
    each(0, W_PARTS, lambda i: wc_copy(0, i).wait_send())
    each(0, W_PARTS, lambda i: wc_copy(1, i).wait_send())
    rg_copy.wait_send()
    pan_copy.wait_send()
    upp_copy.wait_send()
    for d in range(1, 4):
        up_copy(d).wait_send()
        state_copy(d).wait_send()

    def drained(r):
        free_sends(r, lambda copy: copy.wait_send())
        late_sends(r, lambda copy: copy.wait_send())
        for a, zz in ((1, zi), (2, z2), (3, z3)):
            x_forward(a, zz, r).wait_send()

        @pl.when(inner)
        def _():
            z_forward(r).wait_send()

        for d in range(1, 4):
            low_copy(d, r).wait_send()

    each(0, CHUNKS, drained)


def paired_call(args):
    tokens, proj_weight, decay_rate, norm_gain, pool_down, pool_up, span_id, prompt_adapter, owner_pos, slice_len = args
    rows, shard = tokens.shape
    model = proj_weight.shape[1]
    lanes = span_id.shape[1]
    per_owner, _, rank = pool_down.shape
    slice_rows = rows // lanes
    smem = pl.BlockSpec(memory_space=pltpu.SMEM)
    vmem = pl.BlockSpec(memory_space=pltpu.VMEM)
    hbm = pl.BlockSpec(memory_space=pl.ANY)
    dma = pltpu.SemaphoreType.DMA
    bf16, f32 = jnp.bfloat16, jnp.float32
    chunk = slice_rows // CHUNKS
    return pl.pallas_call(
        paired_kernel,
        out_shape=(
            jax.ShapeDtypeStruct((rows, P_SIZE), bf16),
            jax.ShapeDtypeStruct((1, lanes, P_SIZE, P_SIZE), f32),
        ),
        in_specs=[smem, smem, smem, smem, vmem, hbm, hbm, vmem, vmem, vmem],
        out_specs=(vmem, vmem),
        scratch_shapes=[
            pltpu.VMEM((slice_rows, model), bf16),
            pltpu.VMEM((model, 8 * P_SIZE), bf16),
            pltpu.VMEM((per_owner, rank, model), bf16),
            pltpu.VMEM((model // 2, P_SIZE), bf16),
            pltpu.VMEM((2, model // 2, P_SIZE), bf16),
            pltpu.VMEM((model // 2, P_SIZE), bf16),
            pltpu.VMEM((slice_rows, 8 * P_SIZE), f32),
            pltpu.VMEM((chunk, P_SIZE), f32),
            pltpu.VMEM((4, slice_rows // 2, P_SIZE), bf16),
            pltpu.VMEM((4, 2, rank, P_SIZE), bf16),
            pltpu.VMEM((2, 4, 2, rank, P_SIZE), bf16),
            pltpu.VMEM((4, 2, rank, P_SIZE), bf16),
            pltpu.VMEM((4, 2, rank, P_SIZE), bf16),
            pltpu.VMEM((2, 8, P_SIZE), f32),
            pltpu.VMEM((2, slice_rows, P_SIZE), bf16),
            pltpu.VMEM((2, slice_rows, P_SIZE), bf16),
            pltpu.VMEM((2, slice_rows, P_SIZE), f32),
            pltpu.VMEM((2, P_SIZE, P_SIZE), f32),
            pltpu.VMEM((2, 8, P_SIZE), f32),
            pltpu.VMEM((2, P_SIZE + 8, P_SIZE), f32),
            pltpu.VMEM((4, 2, P_SIZE + 8, P_SIZE), f32),
            pltpu.VMEM((2, slice_rows, P_SIZE), bf16),
            pltpu.VMEM((2, P_SIZE, P_SIZE), f32),
            dma((5,)),
            dma,
            dma((3, 2, CHUNKS)),
            dma((8, CHUNKS)),
            dma((4, CHUNKS)),
            dma((W_PARTS,)),
            dma((W_PARTS,)),
            dma((W_PARTS,)),
            dma((W_PARTS,)),
            dma((2, W_PARTS)),
            dma((2, W_PARTS)),
            dma,
            dma,
            dma((2,)),
            dma((4,)),
            dma((4,)),
            dma((4,)),
            dma((4, CHUNKS)),
            dma((4, CHUNKS)),
            dma((4,)),
            dma((4,)),
            dma((2,)),
            dma((2,)),
            dma((2,)),
            dma((2,)),
            dma((2,)),
        ],
        compiler_params=pltpu.CompilerParams(
            collective_id=0, has_side_effects=True, vmem_limit_bytes=58 * 1024 * 1024
        ),
    )(
        span_id.T,
        prompt_adapter,
        owner_pos,
        slice_len.T,
        tokens,
        proj_weight,
        jnp.swapaxes(pool_down, 1, 2),
        pool_up,
        decay_rate.reshape(1, -1),
        norm_gain.reshape(1, -1),
    )


def solution(mesh):
    n, n_seq = mesh.shape["head"], mesh.shape["seq"]

    def body(
        tokens,
        proj_weight,
        decay_rate,
        norm_gain,
        pool_down,
        pool_up,
        span_id,
        prompt_adapter,
        owner_pos,
        slice_len,
    ):
        if n == 8 and n_seq == 4 and span_id.shape[1] == 2:
            return paired_call(
                (
                    tokens,
                    proj_weight,
                    decay_rate,
                    norm_gain,
                    pool_down,
                    pool_up,
                    span_id,
                    prompt_adapter,
                    owner_pos,
                    slice_len,
                )
            )
        rows, shard = tokens.shape
        model = proj_weight.shape[1]
        lanes = span_id.shape[1]
        per_owner, _, rank = pool_down.shape
        slice_rows = rows // lanes
        width = lanes * rank
        smem = pl.BlockSpec(memory_space=pltpu.SMEM)
        vmem = pl.BlockSpec(memory_space=pltpu.VMEM)
        hbm = pl.BlockSpec(memory_space=pl.ANY)
        dma = pltpu.SemaphoreType.DMA
        return pl.pallas_call(
            functools.partial(ring_kernel, n, n_seq),
            out_shape=(
                jax.ShapeDtypeStruct((rows, P_SIZE), jnp.bfloat16),
                jax.ShapeDtypeStruct((1, lanes, P_SIZE, P_SIZE), jnp.float32),
            ),
            in_specs=[smem, smem, smem, smem, vmem, hbm, hbm, vmem, vmem, vmem],
            out_specs=(vmem, vmem),
            scratch_shapes=[
                pltpu.VMEM((2, n // 2, rows, shard), jnp.bfloat16),
                pltpu.VMEM((model, 4 * P_SIZE), jnp.bfloat16),
                pltpu.VMEM((per_owner, model, rank), jnp.bfloat16),
                pltpu.VMEM((per_owner, rank, model), jnp.bfloat16),
                pltpu.VMEM((rows, 4 * P_SIZE), jnp.float32),
                pltpu.VMEM((per_owner, rows, rank), jnp.float32),
                pltpu.VMEM((n, width, P_SIZE), jnp.bfloat16),
                pltpu.VMEM((n, width, P_SIZE), jnp.bfloat16),
                pltpu.VMEM((slice_rows, width), jnp.bfloat16),
                pltpu.VMEM((n, slice_rows // n, width), jnp.bfloat16),
                pltpu.VMEM((n, slice_rows // n, width), jnp.bfloat16),
                pltpu.VMEM((lanes, P_SIZE + 8, P_SIZE), jnp.float32),
                pltpu.VMEM((n_seq, lanes, P_SIZE + 8, P_SIZE), jnp.float32),
                dma((5,)),
                dma((2, n // 2, PIECES)),
                dma((2, n // 2, PIECES)),
                dma((n,)),
                dma((n,)),
                dma((n,)),
                dma((n,)),
                dma((n,)),
                dma((n,)),
                dma((n_seq,)),
                dma((n_seq,)),
            ],
            compiler_params=pltpu.CompilerParams(
                collective_id=0, has_side_effects=True, vmem_limit_bytes=58 * 1024 * 1024
            ),
        )(
            span_id.T,
            prompt_adapter,
            owner_pos,
            slice_len.T,
            tokens,
            proj_weight,
            jnp.swapaxes(pool_down, 1, 2),
            pool_up,
            decay_rate.reshape(1, -1),
            norm_gain.reshape(1, -1),
        )

    in_specs = (
        P("seq", "head"),
        P(None, None, "head"),
        P("head"),
        P("head"),
        P("head", None, None),
        P("head", None, None),
        P(),
        P(),
        P(),
        P(),
    )
    out_specs = (P("seq", "head"), P("seq", None, "head", None))
    return jax.shard_map(body, mesh=mesh, in_specs=in_specs, out_specs=out_specs, check_vma=False)
```

```python
import functools
import math

import jax
import jax.numpy as jnp
from jax import lax
from jax.experimental import pallas as pl
from jax.experimental.pallas import tpu as pltpu
from jax.sharding import PartitionSpec as P

P_SIZE = 128
NORM_FLOOR = 1.0
PIECES = 4
CHUNKS = 4
W_PARTS = 8
LATE = 3
MESH = pl.DeviceIdType.MESH
HIGHEST = lax.Precision.HIGHEST


def grid_of(n):
    across = math.isqrt(n // 2)
    if across >= 2 and 2 * across * across == n:
        return across, n // across
    return 1, n


def head_at(position, n):
    across, depth = grid_of(n)
    if across == 1:
        return position
    width = across - 1
    back = lax.div(lax.div(position, depth) + (across - 1), across)
    rest = (position - depth) * back
    row, step = lax.div(rest, width), lax.rem(rest, width)
    x = 1 + step + lax.rem(row, 2) * (width - 1 - 2 * step)
    return (1 - back) * position * across + back * ((depth - 1 - row) * across + x)


def position_of(head, n):
    across, depth = grid_of(n)
    if across == 1:
        return head
    width = across - 1
    z, x = lax.div(head, across), lax.rem(head, across)
    back = lax.div(x + across - 1, across)
    row, step = depth - 1 - z, (x - 1) * back
    moved = step + lax.rem(row, 2) * (width - 1 - 2 * step)
    return (1 - back) * z + back * (depth + row * width + moved)


def dot(a, b, precision=None):
    return jnp.dot(a, b, preferred_element_type=jnp.float32, precision=precision)


def ring_kernel(
    n,
    n_seq,
    span_ref,
    prompt_ref,
    owner_ref,
    len_ref,
    tok_ref,
    w_hbm,
    down_hbm,
    up_ref,
    rate_ref,
    gain_ref,
    out_ref,
    state_ref,
    slots,
    wbuf,
    dbuf,
    dturn,
    acc,
    lacc,
    up_send,
    up_recv,
    low_send,
    low_recv,
    low_full,
    st_send,
    st_recv,
    w_sem,
    ring_send,
    ring_recv,
    up_ssem,
    up_rsem,
    rs_ssem,
    rs_rsem,
    ag_ssem,
    ag_rsem,
    st_ssem,
    st_rsem,
):
    me = lax.axis_index("head")
    seq = lax.axis_index("seq")
    rows, shard = tok_ref.shape
    lanes = span_ref.shape[0]
    per_owner = down_hbm.shape[0]
    rank = down_hbm.shape[1]
    slice_rows = rows // lanes
    piece = rows // PIECES
    half = n // 2
    here = position_of(me, n)
    right = head_at(lax.rem(here + 1, n), n)
    left = head_at(lax.rem(here + n - 1, n), n)
    toward = (right, left)

    loads = [
        pltpu.make_async_copy(w_hbm.at[c], wbuf.at[:, pl.ds(c * P_SIZE, P_SIZE)], w_sem.at[c])
        for c in range(4)
    ]
    loads.append(pltpu.make_async_copy(down_hbm, dturn, w_sem.at[4]))

    barrier = pltpu.get_barrier_semaphore()

    def greet_head(d, carry):
        pl.semaphore_signal(
            barrier, inc=1, device_id={"head": lax.rem(me + d, n)}, device_id_type=MESH
        )
        return carry

    def greet_seq(d, carry):
        pl.semaphore_signal(
            barrier, inc=1, device_id={"seq": lax.rem(seq + d, n_seq)}, device_id_type=MESH
        )
        return carry

    lax.fori_loop(1, n, greet_head, 0)
    lax.fori_loop(1, n_seq, greet_seq, 0)
    for load in loads:
        load.start()
    pl.semaphore_wait(barrier, n - 1 + n_seq - 1)

    def hop(direction, step, p, own=False):
        span = pl.ds(p * piece, piece)
        source = tok_ref.at[span] if own else slots.at[direction, step - 2, span]
        return pltpu.make_async_remote_copy(
            src_ref=source,
            dst_ref=slots.at[direction, step - 1, span],
            send_sem=ring_send.at[direction, step - 1, p],
            recv_sem=ring_recv.at[direction, step - 1, p],
            device_id={"head": toward[direction]},
            device_id_type=MESH,
        )

    def long_way(direction, p):
        return p % 2 == direction

    for k in range(PIECES):
        for direction in range(2):
            hop(direction, 1, (k + direction) % PIECES, own=True).start()

    places = [owner_ref[prompt_ref[span_ref[j, seq]]] for j in range(lanes)]
    owned = [
        [jnp.where(places[j] == me * per_owner + s, 1.0, 0.0).astype(jnp.float32) for s in range(per_owner)]
        for j in range(lanes)
    ]

    for j in range(lanes):
        mine = sum(owned[j][s] * up_ref[s].astype(jnp.float32) for s in range(per_owner)).astype(jnp.bfloat16)
        for i in range(n):
            up_send[i, pl.ds(j * rank, rank), :] = mine[:, i * P_SIZE : (i + 1) * P_SIZE]

    def up_copy(d):
        peer = lax.rem(me + d, n)
        return pltpu.make_async_remote_copy(
            src_ref=up_send.at[peer],
            dst_ref=up_recv.at[d],
            send_sem=up_ssem.at[d],
            recv_sem=up_rsem.at[d],
            device_id={"head": peer},
            device_id_type=MESH,
        )

    def up_start(d, carry):
        up_copy(d).start()
        return carry

    lax.fori_loop(1, n, up_start, 0)
    up_recv[0] = up_send[me]

    for load in loads:
        load.wait()

    strip = wbuf.shape[0] // 12

    def turn_strip(i, carry):
        deep = pl.ds(pl.multiple_of(i * strip, strip), strip)
        for s in range(per_owner):
            dbuf[s, deep, :] = dturn[s, :, deep].T
        return carry

    lax.fori_loop(0, 12, turn_strip, 0)

    def multiply(x, span, origin, first=False):
        deep = pl.ds(pl.multiple_of(origin * shard, 64), shard)
        gained = dot(x, wbuf[deep, :])
        lows = [dot(x, dbuf[s, deep, :]) for s in range(per_owner)]
        if first:
            acc[span, :] = gained
            for s in range(per_owner):
                lacc[s, span, :] = lows[s]
        else:
            acc[span, :] += gained
            for s in range(per_owner):
                lacc[s, span, :] += lows[s]

    def own_piece(p, carry):
        span = pl.ds(pl.multiple_of(p * piece, piece), piece)
        multiply(tok_ref[span, :], span, me, first=True)
        return carry

    lax.fori_loop(0, PIECES, own_piece, 0)

    def arrive(step, forward, present):
        order = [((k + d) % PIECES, d) for k in range(PIECES) for d in range(2)]
        order = [(p, d) for p, d in order if present(d, p)]
        for p, d in order:
            hop(d, step, p).wait_recv() if not isinstance(step, int) or step > 1 else hop(d, 1, p, own=True).wait_recv()
            if forward(d, p):
                hop(d, step + 1, p).start()
            sign = n - step if d == 0 else step
            origin = head_at(lax.rem(here + sign, n), n)
            span = pl.ds(p * piece, piece)
            multiply(slots[d, step - 1, span, :], span, origin)

    everything = lambda d, p: True
    nothing = lambda d, p: False
    if half >= 2:
        arrive(1, everything if half > 2 else long_way, everything)
    if half > 3:

        def middle(step, carry):
            arrive(step, everything, everything)
            return carry

        lax.fori_loop(2, half - 1, middle, 0)
    if half > 2:
        arrive(half - 1, long_way, everything)
    arrive(half, nothing, long_way)

    width = lanes * rank
    for j in range(lanes):
        span = pl.ds(j * slice_rows, slice_rows)
        mine = sum(owned[j][s] * lacc[s, span, :] for s in range(per_owner)).astype(jnp.bfloat16)
        low_send[:, pl.ds(j * rank, rank)] = mine
    block = slice_rows // n

    def rs_copy(d):
        peer = lax.rem(me + d, n)
        return pltpu.make_async_remote_copy(
            src_ref=low_send.at[pl.ds(pl.multiple_of(peer * block, block), block)],
            dst_ref=low_recv.at[d],
            send_sem=rs_ssem.at[d],
            recv_sem=rs_rsem.at[d],
            device_id={"head": peer},
            device_id_type=MESH,
        )

    def ag_copy(d):
        peer = lax.rem(me + d, n)
        return pltpu.make_async_remote_copy(
            src_ref=low_recv.at[0],
            dst_ref=low_full.at[me],
            send_sem=ag_ssem.at[d],
            recv_sem=ag_rsem.at[d],
            device_id={"head": peer},
            device_id_type=MESH,
        )

    def ag_arrival(d):
        peer = lax.rem(me + n - d, n)
        return pltpu.make_async_remote_copy(
            src_ref=low_recv.at[0],
            dst_ref=low_full.at[peer],
            send_sem=ag_ssem.at[d],
            recv_sem=ag_rsem.at[d],
            device_id={"head": peer},
            device_id_type=MESH,
        )

    def each(count, act):
        def turn(d, carry):
            act(d)
            return carry

        lax.fori_loop(1, count, turn, 0)

    each(n, lambda d: rs_copy(d).start())
    each(n, lambda d: up_copy(d).wait_recv())
    up = jnp.sum(up_recv[...].astype(jnp.float32), axis=0).astype(jnp.bfloat16)
    total = low_send[pl.ds(pl.multiple_of(me * block, block), block), :].astype(jnp.float32)
    each(n, lambda d: rs_copy(d).wait_recv())
    for d in range(1, n):
        total = total + low_recv[d].astype(jnp.float32)
    low_recv[0] = total.astype(jnp.bfloat16)
    each(n, lambda d: ag_copy(d).start())
    low_full[me] = total.astype(jnp.bfloat16)

    slot_ids = lax.broadcasted_iota(jnp.int32, (slice_rows, 1), 0)
    causal = lax.broadcasted_iota(jnp.int32, (slice_rows, slice_rows), 0) >= lax.broadcasted_iota(
        jnp.int32, (slice_rows, slice_rows), 1
    )
    triangle = jnp.where(causal, 1.0, 0.0).astype(jnp.float32)
    columns = lax.broadcasted_iota(jnp.int32, (1, width), 1)
    each(n, lambda d: ag_arrival(d).wait_recv())
    low = low_full[...].reshape(slice_rows, width).astype(jnp.float32)

    kept = []
    for j in range(lanes):
        span = pl.ds(j * slice_rows, slice_rows)
        own = (columns >= j * rank) & (columns < (j + 1) * rank)
        gate = acc[span, pl.ds(3 * P_SIZE, P_SIZE)] + dot(jnp.where(own, low, 0.0).astype(jnp.bfloat16), up)
        live = jnp.where(slot_ids < len_ref[j, seq], 1.0, 0.0).astype(jnp.float32)
        step_log = -(live * rate_ref[...] * (2.0 * jax.nn.sigmoid(gate)))
        cumul = dot(triangle, step_log, HIGHEST)
        query = acc[span, pl.ds(0, P_SIZE)].astype(jnp.bfloat16).astype(jnp.float32)
        key = acc[span, pl.ds(P_SIZE, P_SIZE)].astype(jnp.bfloat16).astype(jnp.float32) * (
            live * P_SIZE ** (-0.5)
        )
        value = acc[span, pl.ds(2 * P_SIZE, P_SIZE)].astype(jnp.bfloat16).astype(jnp.float32)
        last = cumul[slice_rows - 1 :, :]
        carried = lax.dot_general(
            key * jnp.exp(last - cumul),
            value,
            (((0,), (0,)), ((), ())),
            precision=HIGHEST,
            preferred_element_type=jnp.float32,
        )
        st_send[j, pl.ds(0, P_SIZE), :] = carried
        st_send[j, pl.ds(P_SIZE, 8), :] = jnp.broadcast_to(jnp.exp(last), (8, P_SIZE))
        kept.append((live, query * jnp.exp(cumul), key * jnp.exp(-cumul), value))

    def st_copy(d):
        return pltpu.make_async_remote_copy(
            src_ref=st_send,
            dst_ref=st_recv.at[seq],
            send_sem=st_ssem.at[d],
            recv_sem=st_rsem.at[d],
            device_id={"seq": lax.rem(seq + d, n_seq)},
            device_id_type=MESH,
        )

    def st_arrival(d):
        peer = lax.rem(seq + n_seq - d, n_seq)
        return pltpu.make_async_remote_copy(
            src_ref=st_send,
            dst_ref=st_recv.at[peer],
            send_sem=st_ssem.at[d],
            recv_sem=st_rsem.at[d],
            device_id={"seq": peer},
            device_id_type=MESH,
        )

    each(n_seq, lambda d: st_copy(d).start())
    st_recv[seq] = st_send[...]

    inners = []
    for j in range(lanes):
        live, query_decay, key_decay, value = kept[j]
        scores = lax.dot_general(
            query_decay,
            key_decay,
            (((1,), (1,)), ((), ())),
            precision=HIGHEST,
            preferred_element_type=jnp.float32,
        )
        inners.append(dot(jnp.where(causal, scores, 0.0), value, HIGHEST))

    each(n_seq, lambda d: st_arrival(d).wait_recv())
    for j in range(lanes):
        live, query_decay, _, _ = kept[j]
        span = pl.ds(j * slice_rows, slice_rows)
        ended = jnp.zeros((P_SIZE, P_SIZE), jnp.float32)
        start = ended
        final = ended
        for k in range(n_seq):
            if k:
                same = jnp.where(span_ref[j, k] == span_ref[j, k - 1], 1.0, 0.0).astype(jnp.float32)
                begun = same * ended
            else:
                begun = ended
            decay = jnp.broadcast_to(st_recv[k, j, pl.ds(P_SIZE, 1), :], (P_SIZE, P_SIZE)).T
            ended = decay * begun + st_recv[k, j, pl.ds(0, P_SIZE), :]
            at = jnp.where(seq == k, 1.0, 0.0).astype(jnp.float32)
            start = start + at * begun
            final = final + at * ended
        inner = inners[j] + dot(query_decay, start, HIGHEST)
        scale = lax.rsqrt(jnp.maximum(jnp.mean(inner * inner, axis=-1, keepdims=True), NORM_FLOOR))
        out_ref[span, :] = (inner * scale * gain_ref[...] * live).astype(jnp.bfloat16)
        state_ref[0, j] = final

    each(n, lambda d: up_copy(d).wait_send())
    each(n, lambda d: rs_copy(d).wait_send())
    each(n, lambda d: ag_copy(d).wait_send())
    each(n_seq, lambda d: st_copy(d).wait_send())
    for p in range(PIECES):
        for direction in range(2):
            hop(direction, 1, p, own=True).wait_send()
    for direction in range(2):
        for p in range(PIECES):
            reach = half if long_way(direction, p) else half - 1

            def drained(step, carry):
                hop(direction, step, p).wait_send()
                return carry

            lax.fori_loop(2, reach + 1, drained, 0)


def halves(a):
    high = a.astype(jnp.bfloat16)
    return high, (a - high.astype(jnp.float32)).astype(jnp.bfloat16)


def across_rows(a, b):
    return lax.dot_general(a, b, (((1,), (1,)), ((), ())), preferred_element_type=jnp.float32)


def down_rows(a, b):
    return lax.dot_general(a, b, (((0,), (0,)), ((), ())), preferred_element_type=jnp.float32)


def paired_kernel(
    span_ref,
    prompt_ref,
    owner_ref,
    len_ref,
    tok_ref,
    w_hbm,
    down_hbm,
    up_ref,
    rate_ref,
    gain_ref,
    out_ref,
    state_ref,
    tokbuf,
    wbuf,
    dturn,
    dsend,
    din,
    dbuf,
    acc,
    lacc,
    lowb,
    upsend,
    upin,
    upsum,
    upr,
    rgbuf,
    qdh,
    qdl,
    inn,
    run,
    carry,
    st_send,
    st_recv,
    obuf,
    fbuf,
    w_sem,
    t_local,
    t_send,
    t_recv,
    f_send,
    wz_send,
    wz_recv,
    wy_send,
    wy_recv,
    wc_send,
    wc_recv,
    r_send,
    r_recv,
    p_send,
    p_recv,
    u_send,
    u_recv,
    l_send,
    l_recv,
    s_send,
    s_recv,
    o_send,
    o_recv,
    e_send,
    e_recv,
    o_local,
):
    h = lax.axis_index("head")
    s = lax.axis_index("seq")
    z, x = lax.div(h, 2), lax.rem(h, 2)
    y, k = lax.div(s, 2), lax.rem(s, 2)
    b, p = lax.div(z, 2), lax.rem(z, 2)
    zi, z2, z3 = z + 1 - 2 * p, lax.rem(z + 2, 4), 3 - z
    same = k == p
    differ = k != p
    inner = (z == 1) | (z == 2)
    outer = (z == 0) | (z == 3)
    inward = 1 + p
    seqc = 2 * y + p
    lane = k

    rows, shard = tok_ref.shape
    lanes = span_ref.shape[0]
    per_owner, rank, model = down_hbm.shape
    slice_rows = rows // lanes
    chunk = slice_rows // CHUNKS
    deep_part = model // W_PARTS
    wide = 4 * P_SIZE

    def at(xx, yy, zz, kk):
        return {"head": 2 * zz + xx, "seq": 2 * yy + kk}

    def remote(src, dst, send, recv, where):
        return pltpu.make_async_remote_copy(
            src_ref=src, dst_ref=dst, send_sem=send, recv_sem=recv, device_id=where, device_id_type=MESH
        )

    loads = [
        pltpu.make_async_copy(
            w_hbm.at[c],
            wbuf.at[:, pl.ds(pl.multiple_of(p * wide + c * P_SIZE, P_SIZE), P_SIZE)],
            w_sem.at[c],
        )
        for c in range(4)
    ]
    pools = pltpu.make_async_copy(down_hbm, dturn, w_sem.at[4])

    barrier = pltpu.get_barrier_semaphore()
    plane = 2 * h + k

    def greet(d, c):
        other = lax.rem(plane + d, 16)
        where = {"head": lax.div(other, 2), "seq": 2 * y + lax.rem(other, 2)}
        pl.semaphore_signal(barrier, inc=1, device_id=where, device_id_type=MESH)
        return c

    lax.fori_loop(1, 16, greet, 0)
    for zz in (z, zi):
        pl.semaphore_signal(barrier, inc=1, device_id=at(x, 1 - y, zz, k), device_id_type=MESH)
    pools.start()
    rgbuf[p, pl.ds(0, 1), :] = rate_ref[...]
    rgbuf[p, pl.ds(1, 1), :] = gain_ref[...]
    st_recv[...] = jnp.zeros_like(st_recv)
    pl.semaphore_wait(barrier, 17)

    def deep_at(i):
        return pl.ds(pl.multiple_of(i * deep_part, 128), deep_part)

    def col_at(q, c):
        return pl.ds(pl.multiple_of(q * wide + c * P_SIZE, P_SIZE), P_SIZE)

    def wz_copy(i):
        c = 2 * y + k
        return remote(
            w_hbm.at[c, deep_at(i)],
            wbuf.at[deep_at(i), col_at(p, c)],
            wz_send.at[i],
            wz_recv.at[i],
            at(x, y, zi, k),
        )

    def held(i, c):
        return wbuf.at[deep_at(i), col_at(1 - p, c)]

    def wz_arrival(i):
        c = 2 * y + k
        return remote(held(i, c), held(i, c), wz_send.at[i], wz_recv.at[i], at(x, y, zi, k))

    def wy_copy(i):
        c = 2 * y + k
        return remote(held(i, c), held(i, c), wy_send.at[i], wy_recv.at[i], at(x, 1 - y, z, k))

    def wy_arrival(i):
        c = 2 * (1 - y) + k
        return remote(held(i, c), held(i, c), wy_send.at[i], wy_recv.at[i], at(x, 1 - y, z, k))

    def wc_copy(g, i):
        c = 2 * (y + g - 2 * y * g) + k
        return remote(held(i, c), held(i, c), wc_send.at[g, i], wc_recv.at[g, i], at(x, y, z, 1 - k))

    def wc_arrival(g, i):
        c = 2 * (y + g - 2 * y * g) + 1 - k
        return remote(held(i, c), held(i, c), wc_send.at[g, i], wc_recv.at[g, i], at(x, y, z, 1 - k))

    def each(first, count, act):
        def turn(i, c):
            act(i)
            return c

        lax.fori_loop(first, count, turn, 0)

    each(0, 2, lambda i: wz_copy(i).start())

    def mask(seq):
        spot = owner_ref[prompt_ref[span_ref[lane, seq]]]
        return [jnp.where(spot == h * per_owner + i, 1.0, 0.0).astype(jnp.float32) for i in range(per_owner)]

    mine, theirs = mask(seqc), mask(2 * y + 1 - p)
    for g in range(4):
        for q in range(2):
            head = 4 * (g // 2) + 2 * q + g % 2
            part = [up_ref[o, :, head * P_SIZE : (head + 1) * P_SIZE].astype(jnp.float32) for o in range(per_owner)]
            upsend[g, q] = sum(theirs[o] * part[o] for o in range(per_owner)).astype(jnp.bfloat16)
            upsum[g, q] = sum(mine[o] * part[o] for o in range(per_owner)).astype(jnp.bfloat16)

    from_outer = jnp.where(inner, 1, 0)
    pan_copy = remote(dsend, din.at[from_outer], p_send.at[0], p_recv.at[from_outer], at(x, y, inward, k))
    upp_copy = remote(upsend, upin.at[from_outer], p_send.at[1], p_recv.at[2 + from_outer], at(x, y, inward, k))
    upp_copy.start()
    each(2, W_PARTS, lambda i: wz_copy(i).start())
    for load in loads:
        load.start()

    rg_copy = remote(rgbuf.at[p], rgbuf.at[p], r_send, r_recv, at(x, y, zi, k))
    rg_arrival = remote(rgbuf.at[1 - p], rgbuf.at[1 - p], r_send, r_recv, at(x, y, zi, k))
    rg_copy.start()

    def chunk_at(r):
        return pl.ds(pl.multiple_of(r * chunk, chunk), chunk)

    def place(f, r):
        return tokbuf.at[chunk_at(r), pl.ds(pl.multiple_of(f * shard, 128), shard)]

    def tok_copy(t, j, r, where):
        source = tok_ref.at[pl.ds(pl.multiple_of(j * slice_rows + r * chunk, chunk), chunk)]
        return remote(source, place(h, r), t_send.at[t, j, r], t_recv.at[h, r], where)

    def free_sends(r, act):
        @pl.when(same)
        def _():
            act(tok_copy(0, 1 - k, r, at(x, y, z, 1 - k)))
            for j in range(2):
                act(tok_copy(1, j, r, at(1 - x, y, z, j)))

        @pl.when(differ & inner)
        def _():
            for j in range(2):
                act(tok_copy(2, j, r, at(x, y, z3, j)))

    def late_sends(r, act):
        @pl.when(same)
        def _():
            for j in range(2):
                act(tok_copy(2, j, r, at(x, y, z2, j)))

        @pl.when(differ)
        def _():
            for j in range(2):
                act(tok_copy(1, j, r, at(x, y, zi, j)))

    own = pltpu.make_async_copy(
        tok_ref.at[pl.ds(pl.multiple_of(lane * slice_rows, chunk), slice_rows)],
        tokbuf.at[:, pl.ds(pl.multiple_of(h * shard, 128), shard)],
        t_local,
    )

    each(0, CHUNKS, lambda r: free_sends(r, lambda copy: copy.start()))

    @pl.when(same)
    def _():
        own.start()

    pools.wait()
    half_model = model // 2
    strips = 6
    strip = half_model // strips

    def strip_at(i, base=0):
        return pl.ds(pl.multiple_of(base + i * strip, 128), strip)

    def pick(weights, i):
        both = [
            sum(weights[o] * dturn[o, :, strip_at(i, base)].astype(jnp.float32) for o in range(per_owner))
            for base in (0, half_model)
        ]
        return jnp.concatenate(both, axis=0).astype(jnp.bfloat16).T

    def fill(i):
        dsend[strip_at(i), :] = pick(theirs, i)
        dbuf[strip_at(i), :] = pick(mine, i)

    each(0, strips, fill)

    def arrived(f, r):
        remote(place(f, r), place(f, r), t_send.at[0, 0, 0], t_recv.at[f, r], at(1 - x, y, z, k)).wait_recv()

    def x_forward(a, zz, r):
        f = 2 * zz + x
        return remote(place(f, r), place(f, r), f_send.at[a - 1, r], t_recv.at[f, r], at(1 - x, y, z, k))

    def z_forward(r):
        f = 2 * zi + x
        return remote(place(f, r), place(f, r), f_send.at[3, r], t_recv.at[f, r], at(x, y, z2, k))

    @pl.when(inner)
    def _():
        pan_copy.start()

    mates = [None, at(1 - x, y, z, k), at(x, y, z2, k), at(1 - x, y, z2, k)]
    groups = [2 * b + x, 2 * b + 1 - x, 2 * (1 - b) + x, 2 * (1 - b) + 1 - x]

    def up_copy(d):
        return remote(upsum.at[groups[d]], upr.at[d], u_send.at[d], u_recv.at[d], mates[d])

    @pl.when(outer)
    def _():
        for d in range(1, 4):
            up_copy(d).start()

    def spread(i, c):
        wz_arrival(i).wait_recv()
        wy_copy(i).start()
        wc_copy(0, i).start()

        @pl.when(i > 0)
        def _():
            wy_arrival(i - 1).wait_recv()
            wc_copy(1, i - 1).start()

        @pl.when(inner & (lax.rem(i, W_PARTS // CHUNKS) == 0))
        def _():
            r = lax.div(i, W_PARTS // CHUNKS)
            arrived(2 * z3 + x, r)
            x_forward(3, z3, r).start()

        @pl.when(inner & (i == 4))
        def _():
            whole = upsum[...].astype(jnp.float32)
            for g in range(2):
                remote(upsend, upin.at[g], p_send.at[1], p_recv.at[2 + g], at(x, y, zi, k)).wait_recv()
                whole = whole + upin[g].astype(jnp.float32)
            upsum[...] = whole.astype(jnp.bfloat16)
            for d in range(1, 4):
                up_copy(d).start()

        @pl.when((i == LATE) & outer)
        def _():
            pan_copy.start()

        @pl.when(i == LATE)
        def _():
            each(0, CHUNKS, lambda r: late_sends(r, lambda copy: copy.start()))

        @pl.when(outer & (i >= W_PARTS - CHUNKS))
        def _():
            r = i - (W_PARTS - CHUNKS)
            arrived(2 * z2 + x, r)
            x_forward(2, z2, r).start()

        return c

    lax.fori_loop(0, W_PARTS, spread, 0)
    wy_arrival(W_PARTS - 1).wait_recv()
    wc_copy(1, W_PARTS - 1).start()

    def gather_down():
        @pl.when(inner)
        def _():
            for g in range(2):
                remote(dsend, din.at[g], p_send.at[0], p_recv.at[g], at(x, y, zi, k)).wait_recv()

            def turn(i):
                whole = dbuf[strip_at(i), :].astype(jnp.float32)
                for g in range(2):
                    whole = whole + din[g, strip_at(i), :].astype(jnp.float32)
                dbuf[strip_at(i), :] = whole.astype(jnp.bfloat16)

            each(0, strips, turn)

    upr[0] = upsum[groups[0]]

    def packed_at(r):
        return pl.ds(pl.multiple_of(r * (chunk // 2), chunk // 2), chunk // 2)

    def low_copy(d, r):
        span = packed_at(r)
        return remote(lowb.at[0, span], lowb.at[d, span], l_send.at[d, r], l_recv.at[d, r], mates[d])

    run[...] = jnp.zeros_like(run)
    carry[...] = jnp.zeros_like(carry)

    def shard_of(a, column):
        high, bit = lax.div(a, 2), lax.rem(a, 2)
        zz = 2 * (b + high - 2 * b * high) + p + bit - 2 * p * bit
        return 2 * zz + column

    low_half = lax.div(lax.broadcasted_iota(jnp.int32, (1, P_SIZE), 1), rank)

    def multiply(f, r, first):
        span = chunk_at(r)
        deep = pl.ds(pl.multiple_of(f * shard, 128), shard)
        block = tokbuf[span, deep]
        late = lax.div(f, 4)
        packed = pl.ds(pl.multiple_of((f - 4 * late) * shard, 128), shard)
        low_part = jnp.where(low_half == late, dot(block, dbuf[packed, :]), 0.0)
        part = dot(block, wbuf[deep, :])

        @pl.when(first)
        def _():
            lacc[...] = low_part
            acc[span, :] = part

        @pl.when(jnp.logical_not(first))
        def _():
            lacc[...] += low_part
            acc[span, :] += part

    def onward(a, zz, r):
        arrived(2 * zz + x, r)
        x_forward(a, zz, r).start()

    def advance(r):
        @pl.when(inner)
        def _():
            onward(1, zi, r)
            z_forward(r).start()
            onward(2, z2, r)

        @pl.when(outer)
        def _():
            onward(3, z3, r)

            @pl.when(r + 2 < CHUNKS)
            def _():
                onward(1, zi, r + 2)

        @pl.when(differ)
        def _():
            arrived(h, r)

        @pl.when(same & (r == 0))
        def _():
            own.wait()

    soon = jnp.where(inner, 3, 2)

    def other(a, r):
        f = shard_of(a, 1 - x)
        arrived(f, r)
        multiply(f, r, a < 0)

    def early(r):
        each(0, 4, lambda a: multiply(shard_of(a, x), r, a == 0))
        each(0, 2, lambda i: other(i * soon, r))

    def finish(r):
        second, step_to = jnp.where(inner, 2, 1), jnp.where(inner, -1, 2)
        each(0, 2, lambda i: other(second + i * step_to, r))
        low_sum = (lacc[:, :rank] + lacc[:, rank:]).astype(jnp.bfloat16)
        lowb[0, packed_at(r), :] = jnp.concatenate([low_sum[: chunk // 2], low_sum[chunk // 2 :]], axis=1)
        for d in (3, 2, 1):
            low_copy(d, r).start()

    row_ids = lax.broadcasted_iota(jnp.int32, (chunk, chunk), 0)
    column_ids = lax.broadcasted_iota(jnp.int32, (chunk, chunk), 1)
    causal = row_ids >= column_ids
    triangle = jnp.where(causal, 1.0, 0.0).astype(jnp.bfloat16)
    slot_ids = lax.broadcasted_iota(jnp.int32, (slice_rows, 1), 0)
    chunk_ids = lax.broadcasted_iota(jnp.int32, (chunk, 1), 0)
    length = len_ref[lane, seqc]

    def state_copy(d):
        where = [None, at(x, 1 - y, z, k), at(x, y, zi, k), at(x, 1 - y, zi, k)][d]
        return remote(st_send, st_recv.at[seqc], s_send.at[d], s_recv.at[d], where)

    def later(d, act, side=0):
        pl.when((p if d == 2 else y) == side)(lambda: act())

    def state_arrival(d):
        yy, pp = [None, (1 - y, p), (y, 1 - p), (1 - y, 1 - p)][d]
        return remote(st_send, st_recv.at[2 * yy + pp], s_send.at[d], s_recv.at[d], at(x, 1 - y, z, k))

    def attend(r):
        span = chunk_at(r)

        @pl.when(r == 0)
        def _():
            for d in range(1, 4):
                up_copy(d).wait_recv()
            for q in range(2):
                upr[0, q] = sum(upr[d, q].astype(jnp.float32) for d in range(4)).astype(jnp.bfloat16)

        for d in range(1, 4):
            low_copy(d, r).wait_recv()
        low = sum(lowb[d, packed_at(r), :].astype(jnp.float32) for d in range(4)).astype(jnp.bfloat16)
        low = jnp.concatenate([low[:, :rank], low[:, rank:]], axis=0)
        live = jnp.where(chunk_ids + r * chunk < length, 1.0, 0.0).astype(jnp.float32)
        kept = []
        for q in range(2):
            first = q * wide
            gate = acc[span, first + 3 * P_SIZE : first + 4 * P_SIZE] + dot(low, upr[0, q])
            step_log = -(live * rgbuf[q, pl.ds(0, 1), :] * (2.0 * jax.nn.sigmoid(gate)))
            a0, rest = halves(step_log)[0], step_log
            rest = rest - a0.astype(jnp.float32)
            a1, a2 = halves(rest)
            cumul = dot(triangle, a0) + (dot(triangle, a1) + dot(triangle, a2)) + carry[q, pl.ds(0, 1), :]
            carry[q] = jnp.broadcast_to(cumul[chunk - 1 :, :], (8, P_SIZE))
            query = acc[span, first : first + P_SIZE].astype(jnp.bfloat16).astype(jnp.float32)
            key = acc[span, first + P_SIZE : first + 2 * P_SIZE].astype(jnp.bfloat16).astype(jnp.float32) * (
                live * P_SIZE ** (-0.5)
            )
            value = acc[span, first + 2 * P_SIZE : first + 3 * P_SIZE].astype(jnp.bfloat16)
            q_high, q_low = halves(query * jnp.exp(cumul))
            k_high, k_low = halves(key * jnp.exp(-cumul))
            qdh[q, span, :] = q_high
            qdl[q, span, :] = q_low
            before = run[q]
            run[q] = before + (down_rows(k_high, value) + down_rows(k_low, value))
            kept.append((q_high, q_low, k_high, k_low, value, before))

        @pl.when(r == CHUNKS - 1)
        def _():
            for q in range(2):
                st_send[q, pl.ds(0, P_SIZE), :] = run[q]
                st_send[q, pl.ds(P_SIZE, 8), :] = jnp.exp(carry[q])
            for d in (3, 1, 2):
                later(d, state_copy(d).start)
            st_recv[seqc] = st_send[...]

        for q in range(2):
            q_high, q_low, k_high, k_low, value, before = kept[q]
            scores = across_rows(q_high, k_high) + (across_rows(q_high, k_low) + across_rows(q_low, k_high))
            s_high, s_low = halves(jnp.where(causal, scores, 0.0))
            b_high, b_low = halves(before)
            inn[q, span, :] = (
                dot(s_high, value)
                + dot(s_low, value)
                + dot(q_high, b_high)
                + (dot(q_high, b_low) + dot(q_low, b_high))
            )

    @pl.when(outer)
    def _():
        each(0, 2, lambda r: onward(1, zi, r))

    for i in range(4):
        loads[i].wait()
    each(0, W_PARTS, lambda i: wc_arrival(0, i).wait_recv())
    each(0, W_PARTS, lambda i: wc_arrival(1, i).wait_recv())
    rg_arrival.wait_recv()
    def step(t, c):
        @pl.when(t < CHUNKS)
        def _():
            advance(t)

        @pl.when(t == 0)
        def _():
            gather_down()

        @pl.when((t > 0) & (t <= CHUNKS))
        def _():
            finish(t - 1)

        @pl.when(t < CHUNKS)
        def _():
            early(t)

        @pl.when(t > 2)
        def _():
            attend(t - 3)

        return c

    lax.fori_loop(0, CHUNKS + 3, step, 0)

    for d in range(1, 4):
        later(d, state_arrival(d).wait_recv, 1)
    alive = jnp.where(slot_ids < length, 1.0, 0.0).astype(jnp.float32)

    def out_copy(q, where):
        return remote(
            obuf.at[q],
            out_ref.at[pl.ds(pl.multiple_of(lane * slice_rows, chunk), slice_rows)],
            o_send.at[q],
            o_recv.at[lane],
            where,
        )

    def end_copy(q, where):
        return remote(fbuf.at[q], state_ref.at[0, lane], e_send.at[q], e_recv.at[lane], where)

    keep_out = pltpu.make_async_copy(
        obuf.at[p], out_ref.at[pl.ds(pl.multiple_of(lane * slice_rows, chunk), slice_rows)], o_local.at[0]
    )
    keep_end = pltpu.make_async_copy(fbuf.at[p], state_ref.at[0, lane], o_local.at[1])
    away, beside = at(x, y, zi, p), at(x, y, z, 1 - k)

    for i in range(2):
        q = 1 - p if i == 0 else p
        ended = jnp.zeros((P_SIZE, P_SIZE), jnp.float32)
        start = ended
        final = ended
        for g in range(4):
            if g:
                kin = jnp.where(span_ref[lane, g] == span_ref[lane, g - 1], 1.0, 0.0).astype(jnp.float32)
                begun = kin * ended
            else:
                begun = ended
            decay = jnp.broadcast_to(st_recv[g, q, pl.ds(P_SIZE, 1), :], (P_SIZE, P_SIZE)).T
            ended = decay * (begun + st_recv[g, q, pl.ds(0, P_SIZE), :])
            now = jnp.where(seqc == g, 1.0, 0.0).astype(jnp.float32)
            start = start + now * begun
            final = final + now * ended
        fbuf[q] = final
        b_high, b_low = halves(start)
        total = inn[q] + dot(qdh[q], b_high) + (dot(qdh[q], b_low) + dot(qdl[q], b_high))
        scale = lax.rsqrt(jnp.maximum(jnp.mean(total * total, axis=-1, keepdims=True), NORM_FLOOR))
        obuf[q] = (total * scale * rgbuf[q, pl.ds(1, 1), :] * alive).astype(jnp.bfloat16)
        if i == 0:
            end_copy(q, away).start()
            out_copy(q, away).start()
        else:

            @pl.when(same)
            def _():
                keep_end.start()
                keep_out.start()

            @pl.when(differ)
            def _():
                end_copy(p, beside).start()
                out_copy(p, beside).start()

    def landed(j):
        span = pl.ds(pl.multiple_of(j * slice_rows, chunk), slice_rows)
        remote(obuf.at[0], out_ref.at[span], o_send.at[0], o_recv.at[j], beside).wait_recv()
        remote(fbuf.at[0], state_ref.at[0, j], e_send.at[0], e_recv.at[j], beside).wait_recv()

    landed(1 - k)

    @pl.when(same)
    def _():
        keep_end.wait()
        keep_out.wait()

    @pl.when(differ)
    def _():
        landed(k)
        end_copy(p, beside).wait_send()
        out_copy(p, beside).wait_send()

    end_copy(1 - p, away).wait_send()
    out_copy(1 - p, away).wait_send()
    each(0, W_PARTS, lambda i: wz_copy(i).wait_send())
    each(0, W_PARTS, lambda i: wy_copy(i).wait_send())
    each(0, W_PARTS, lambda i: wc_copy(0, i).wait_send())
    each(0, W_PARTS, lambda i: wc_copy(1, i).wait_send())
    rg_copy.wait_send()
    pan_copy.wait_send()
    upp_copy.wait_send()
    for d in range(1, 4):
        up_copy(d).wait_send()
        later(d, state_copy(d).wait_send)

    def drained(r):
        free_sends(r, lambda copy: copy.wait_send())
        late_sends(r, lambda copy: copy.wait_send())
        for a, zz in ((1, zi), (2, z2), (3, z3)):
            x_forward(a, zz, r).wait_send()

        @pl.when(inner)
        def _():
            z_forward(r).wait_send()

        for d in range(1, 4):
            low_copy(d, r).wait_send()

    each(0, CHUNKS, drained)


def paired_call(args):
    tokens, proj_weight, decay_rate, norm_gain, pool_down, pool_up, span_id, prompt_adapter, owner_pos, slice_len = args
    rows, shard = tokens.shape
    model = proj_weight.shape[1]
    lanes = span_id.shape[1]
    per_owner, _, rank = pool_down.shape
    slice_rows = rows // lanes
    smem = pl.BlockSpec(memory_space=pltpu.SMEM)
    vmem = pl.BlockSpec(memory_space=pltpu.VMEM)
    hbm = pl.BlockSpec(memory_space=pl.ANY)
    dma = pltpu.SemaphoreType.DMA
    bf16, f32 = jnp.bfloat16, jnp.float32
    chunk = slice_rows // CHUNKS
    return pl.pallas_call(
        paired_kernel,
        out_shape=(
            jax.ShapeDtypeStruct((rows, P_SIZE), bf16),
            jax.ShapeDtypeStruct((1, lanes, P_SIZE, P_SIZE), f32),
        ),
        in_specs=[smem, smem, smem, smem, vmem, hbm, hbm, vmem, vmem, vmem],
        out_specs=(vmem, vmem),
        scratch_shapes=[
            pltpu.VMEM((slice_rows, model), bf16),
            pltpu.VMEM((model, 8 * P_SIZE), bf16),
            pltpu.VMEM((per_owner, rank, model), bf16),
            pltpu.VMEM((model // 2, P_SIZE), bf16),
            pltpu.VMEM((2, model // 2, P_SIZE), bf16),
            pltpu.VMEM((model // 2, P_SIZE), bf16),
            pltpu.VMEM((slice_rows, 8 * P_SIZE), f32),
            pltpu.VMEM((chunk, P_SIZE), f32),
            pltpu.VMEM((4, slice_rows // 2, P_SIZE), bf16),
            pltpu.VMEM((4, 2, rank, P_SIZE), bf16),
            pltpu.VMEM((2, 4, 2, rank, P_SIZE), bf16),
            pltpu.VMEM((4, 2, rank, P_SIZE), bf16),
            pltpu.VMEM((4, 2, rank, P_SIZE), bf16),
            pltpu.VMEM((2, 8, P_SIZE), f32),
            pltpu.VMEM((2, slice_rows, P_SIZE), bf16),
            pltpu.VMEM((2, slice_rows, P_SIZE), bf16),
            pltpu.VMEM((2, slice_rows, P_SIZE), f32),
            pltpu.VMEM((2, P_SIZE, P_SIZE), f32),
            pltpu.VMEM((2, 8, P_SIZE), f32),
            pltpu.VMEM((2, P_SIZE + 8, P_SIZE), f32),
            pltpu.VMEM((4, 2, P_SIZE + 8, P_SIZE), f32),
            pltpu.VMEM((2, slice_rows, P_SIZE), bf16),
            pltpu.VMEM((2, P_SIZE, P_SIZE), f32),
            dma((5,)),
            dma,
            dma((3, 2, CHUNKS)),
            dma((8, CHUNKS)),
            dma((4, CHUNKS)),
            dma((W_PARTS,)),
            dma((W_PARTS,)),
            dma((W_PARTS,)),
            dma((W_PARTS,)),
            dma((2, W_PARTS)),
            dma((2, W_PARTS)),
            dma,
            dma,
            dma((2,)),
            dma((4,)),
            dma((4,)),
            dma((4,)),
            dma((4, CHUNKS)),
            dma((4, CHUNKS)),
            dma((4,)),
            dma((4,)),
            dma((2,)),
            dma((2,)),
            dma((2,)),
            dma((2,)),
            dma((2,)),
        ],
        compiler_params=pltpu.CompilerParams(
            collective_id=0, has_side_effects=True, vmem_limit_bytes=58 * 1024 * 1024
        ),
    )(
        span_id.T,
        prompt_adapter,
        owner_pos,
        slice_len.T,
        tokens,
        proj_weight,
        jnp.swapaxes(pool_down, 1, 2),
        pool_up,
        decay_rate.reshape(1, -1),
        norm_gain.reshape(1, -1),
    )


def solution(mesh):
    n, n_seq = mesh.shape["head"], mesh.shape["seq"]

    def body(
        tokens,
        proj_weight,
        decay_rate,
        norm_gain,
        pool_down,
        pool_up,
        span_id,
        prompt_adapter,
        owner_pos,
        slice_len,
    ):
        if n == 8 and n_seq == 4 and span_id.shape[1] == 2:
            return paired_call(
                (
                    tokens,
                    proj_weight,
                    decay_rate,
                    norm_gain,
                    pool_down,
                    pool_up,
                    span_id,
                    prompt_adapter,
                    owner_pos,
                    slice_len,
                )
            )
        rows, shard = tokens.shape
        model = proj_weight.shape[1]
        lanes = span_id.shape[1]
        per_owner, _, rank = pool_down.shape
        slice_rows = rows // lanes
        width = lanes * rank
        smem = pl.BlockSpec(memory_space=pltpu.SMEM)
        vmem = pl.BlockSpec(memory_space=pltpu.VMEM)
        hbm = pl.BlockSpec(memory_space=pl.ANY)
        dma = pltpu.SemaphoreType.DMA
        return pl.pallas_call(
            functools.partial(ring_kernel, n, n_seq),
            out_shape=(
                jax.ShapeDtypeStruct((rows, P_SIZE), jnp.bfloat16),
                jax.ShapeDtypeStruct((1, lanes, P_SIZE, P_SIZE), jnp.float32),
            ),
            in_specs=[smem, smem, smem, smem, vmem, hbm, hbm, vmem, vmem, vmem],
            out_specs=(vmem, vmem),
            scratch_shapes=[
                pltpu.VMEM((2, n // 2, rows, shard), jnp.bfloat16),
                pltpu.VMEM((model, 4 * P_SIZE), jnp.bfloat16),
                pltpu.VMEM((per_owner, model, rank), jnp.bfloat16),
                pltpu.VMEM((per_owner, rank, model), jnp.bfloat16),
                pltpu.VMEM((rows, 4 * P_SIZE), jnp.float32),
                pltpu.VMEM((per_owner, rows, rank), jnp.float32),
                pltpu.VMEM((n, width, P_SIZE), jnp.bfloat16),
                pltpu.VMEM((n, width, P_SIZE), jnp.bfloat16),
                pltpu.VMEM((slice_rows, width), jnp.bfloat16),
                pltpu.VMEM((n, slice_rows // n, width), jnp.bfloat16),
                pltpu.VMEM((n, slice_rows // n, width), jnp.bfloat16),
                pltpu.VMEM((lanes, P_SIZE + 8, P_SIZE), jnp.float32),
                pltpu.VMEM((n_seq, lanes, P_SIZE + 8, P_SIZE), jnp.float32),
                dma((5,)),
                dma((2, n // 2, PIECES)),
                dma((2, n // 2, PIECES)),
                dma((n,)),
                dma((n,)),
                dma((n,)),
                dma((n,)),
                dma((n,)),
                dma((n,)),
                dma((n_seq,)),
                dma((n_seq,)),
            ],
            compiler_params=pltpu.CompilerParams(
                collective_id=0, has_side_effects=True, vmem_limit_bytes=58 * 1024 * 1024
            ),
        )(
            span_id.T,
            prompt_adapter,
            owner_pos,
            slice_len.T,
            tokens,
            proj_weight,
            jnp.swapaxes(pool_down, 1, 2),
            pool_up,
            decay_rate.reshape(1, -1),
            norm_gain.reshape(1, -1),
        )

    in_specs = (
        P("seq", "head"),
        P(None, None, "head"),
        P("head"),
        P("head"),
        P("head", None, None),
        P("head", None, None),
        P(),
        P(),
        P(),
        P(),
    )
    out_specs = (P("seq", "head"), P("seq", None, "head", None))
    return jax.shard_map(body, mesh=mesh, in_specs=in_specs, out_specs=out_specs, check_vma=False)
```

```python
import functools
import math

import jax
import jax.numpy as jnp
from jax import lax
from jax.experimental import pallas as pl
from jax.experimental.pallas import tpu as pltpu
from jax.sharding import PartitionSpec as P

P_SIZE = 128
NORM_FLOOR = 1.0
PIECES = 4
CHUNKS = 2
W_PARTS = 8
LATE = 3
MESH = pl.DeviceIdType.MESH
HIGHEST = lax.Precision.HIGHEST


def grid_of(n):
    across = math.isqrt(n // 2)
    if across >= 2 and 2 * across * across == n:
        return across, n // across
    return 1, n


def head_at(position, n):
    across, depth = grid_of(n)
    if across == 1:
        return position
    width = across - 1
    back = lax.div(lax.div(position, depth) + (across - 1), across)
    rest = (position - depth) * back
    row, step = lax.div(rest, width), lax.rem(rest, width)
    x = 1 + step + lax.rem(row, 2) * (width - 1 - 2 * step)
    return (1 - back) * position * across + back * ((depth - 1 - row) * across + x)


def position_of(head, n):
    across, depth = grid_of(n)
    if across == 1:
        return head
    width = across - 1
    z, x = lax.div(head, across), lax.rem(head, across)
    back = lax.div(x + across - 1, across)
    row, step = depth - 1 - z, (x - 1) * back
    moved = step + lax.rem(row, 2) * (width - 1 - 2 * step)
    return (1 - back) * z + back * (depth + row * width + moved)


def dot(a, b, precision=None):
    return jnp.dot(a, b, preferred_element_type=jnp.float32, precision=precision)


def ring_kernel(
    n,
    n_seq,
    span_ref,
    prompt_ref,
    owner_ref,
    len_ref,
    tok_ref,
    w_hbm,
    down_hbm,
    up_ref,
    rate_ref,
    gain_ref,
    out_ref,
    state_ref,
    slots,
    wbuf,
    dbuf,
    dturn,
    acc,
    lacc,
    up_send,
    up_recv,
    low_send,
    low_recv,
    low_full,
    st_send,
    st_recv,
    w_sem,
    ring_send,
    ring_recv,
    up_ssem,
    up_rsem,
    rs_ssem,
    rs_rsem,
    ag_ssem,
    ag_rsem,
    st_ssem,
    st_rsem,
):
    me = lax.axis_index("head")
    seq = lax.axis_index("seq")
    rows, shard = tok_ref.shape
    lanes = span_ref.shape[0]
    per_owner = down_hbm.shape[0]
    rank = down_hbm.shape[1]
    slice_rows = rows // lanes
    piece = rows // PIECES
    half = n // 2
    here = position_of(me, n)
    right = head_at(lax.rem(here + 1, n), n)
    left = head_at(lax.rem(here + n - 1, n), n)
    toward = (right, left)

    loads = [
        pltpu.make_async_copy(w_hbm.at[c], wbuf.at[:, pl.ds(c * P_SIZE, P_SIZE)], w_sem.at[c])
        for c in range(4)
    ]
    loads.append(pltpu.make_async_copy(down_hbm, dturn, w_sem.at[4]))

    barrier = pltpu.get_barrier_semaphore()

    def greet_head(d, carry):
        pl.semaphore_signal(
            barrier, inc=1, device_id={"head": lax.rem(me + d, n)}, device_id_type=MESH
        )
        return carry

    def greet_seq(d, carry):
        pl.semaphore_signal(
            barrier, inc=1, device_id={"seq": lax.rem(seq + d, n_seq)}, device_id_type=MESH
        )
        return carry

    lax.fori_loop(1, n, greet_head, 0)
    lax.fori_loop(1, n_seq, greet_seq, 0)
    for load in loads:
        load.start()
    pl.semaphore_wait(barrier, n - 1 + n_seq - 1)

    def hop(direction, step, p, own=False):
        span = pl.ds(p * piece, piece)
        source = tok_ref.at[span] if own else slots.at[direction, step - 2, span]
        return pltpu.make_async_remote_copy(
            src_ref=source,
            dst_ref=slots.at[direction, step - 1, span],
            send_sem=ring_send.at[direction, step - 1, p],
            recv_sem=ring_recv.at[direction, step - 1, p],
            device_id={"head": toward[direction]},
            device_id_type=MESH,
        )

    def long_way(direction, p):
        return p % 2 == direction

    for k in range(PIECES):
        for direction in range(2):
            hop(direction, 1, (k + direction) % PIECES, own=True).start()

    places = [owner_ref[prompt_ref[span_ref[j, seq]]] for j in range(lanes)]
    owned = [
        [jnp.where(places[j] == me * per_owner + s, 1.0, 0.0).astype(jnp.float32) for s in range(per_owner)]
        for j in range(lanes)
    ]

    for j in range(lanes):
        mine = sum(owned[j][s] * up_ref[s].astype(jnp.float32) for s in range(per_owner)).astype(jnp.bfloat16)
        for i in range(n):
            up_send[i, pl.ds(j * rank, rank), :] = mine[:, i * P_SIZE : (i + 1) * P_SIZE]

    def up_copy(d):
        peer = lax.rem(me + d, n)
        return pltpu.make_async_remote_copy(
            src_ref=up_send.at[peer],
            dst_ref=up_recv.at[d],
            send_sem=up_ssem.at[d],
            recv_sem=up_rsem.at[d],
            device_id={"head": peer},
            device_id_type=MESH,
        )

    def up_start(d, carry):
        up_copy(d).start()
        return carry

    lax.fori_loop(1, n, up_start, 0)
    up_recv[0] = up_send[me]

    for load in loads:
        load.wait()

    strip = wbuf.shape[0] // 12

    def turn_strip(i, carry):
        deep = pl.ds(pl.multiple_of(i * strip, strip), strip)
        for s in range(per_owner):
            dbuf[s, deep, :] = dturn[s, :, deep].T
        return carry

    lax.fori_loop(0, 12, turn_strip, 0)

    def multiply(x, span, origin, first=False):
        deep = pl.ds(pl.multiple_of(origin * shard, 64), shard)
        gained = dot(x, wbuf[deep, :])
        lows = [dot(x, dbuf[s, deep, :]) for s in range(per_owner)]
        if first:
            acc[span, :] = gained
            for s in range(per_owner):
                lacc[s, span, :] = lows[s]
        else:
            acc[span, :] += gained
            for s in range(per_owner):
                lacc[s, span, :] += lows[s]

    def own_piece(p, carry):
        span = pl.ds(pl.multiple_of(p * piece, piece), piece)
        multiply(tok_ref[span, :], span, me, first=True)
        return carry

    lax.fori_loop(0, PIECES, own_piece, 0)

    def arrive(step, forward, present):
        order = [((k + d) % PIECES, d) for k in range(PIECES) for d in range(2)]
        order = [(p, d) for p, d in order if present(d, p)]
        for p, d in order:
            hop(d, step, p).wait_recv() if not isinstance(step, int) or step > 1 else hop(d, 1, p, own=True).wait_recv()
            if forward(d, p):
                hop(d, step + 1, p).start()
            sign = n - step if d == 0 else step
            origin = head_at(lax.rem(here + sign, n), n)
            span = pl.ds(p * piece, piece)
            multiply(slots[d, step - 1, span, :], span, origin)

    everything = lambda d, p: True
    nothing = lambda d, p: False
    if half >= 2:
        arrive(1, everything if half > 2 else long_way, everything)
    if half > 3:

        def middle(step, carry):
            arrive(step, everything, everything)
            return carry

        lax.fori_loop(2, half - 1, middle, 0)
    if half > 2:
        arrive(half - 1, long_way, everything)
    arrive(half, nothing, long_way)

    width = lanes * rank
    for j in range(lanes):
        span = pl.ds(j * slice_rows, slice_rows)
        mine = sum(owned[j][s] * lacc[s, span, :] for s in range(per_owner)).astype(jnp.bfloat16)
        low_send[:, pl.ds(j * rank, rank)] = mine
    block = slice_rows // n

    def rs_copy(d):
        peer = lax.rem(me + d, n)
        return pltpu.make_async_remote_copy(
            src_ref=low_send.at[pl.ds(pl.multiple_of(peer * block, block), block)],
            dst_ref=low_recv.at[d],
            send_sem=rs_ssem.at[d],
            recv_sem=rs_rsem.at[d],
            device_id={"head": peer},
            device_id_type=MESH,
        )

    def ag_copy(d):
        peer = lax.rem(me + d, n)
        return pltpu.make_async_remote_copy(
            src_ref=low_recv.at[0],
            dst_ref=low_full.at[me],
            send_sem=ag_ssem.at[d],
            recv_sem=ag_rsem.at[d],
            device_id={"head": peer},
            device_id_type=MESH,
        )

    def ag_arrival(d):
        peer = lax.rem(me + n - d, n)
        return pltpu.make_async_remote_copy(
            src_ref=low_recv.at[0],
            dst_ref=low_full.at[peer],
            send_sem=ag_ssem.at[d],
            recv_sem=ag_rsem.at[d],
            device_id={"head": peer},
            device_id_type=MESH,
        )

    def each(count, act):
        def turn(d, carry):
            act(d)
            return carry

        lax.fori_loop(1, count, turn, 0)

    each(n, lambda d: rs_copy(d).start())
    each(n, lambda d: up_copy(d).wait_recv())
    up = jnp.sum(up_recv[...].astype(jnp.float32), axis=0).astype(jnp.bfloat16)
    total = low_send[pl.ds(pl.multiple_of(me * block, block), block), :].astype(jnp.float32)
    each(n, lambda d: rs_copy(d).wait_recv())
    for d in range(1, n):
        total = total + low_recv[d].astype(jnp.float32)
    low_recv[0] = total.astype(jnp.bfloat16)
    each(n, lambda d: ag_copy(d).start())
    low_full[me] = total.astype(jnp.bfloat16)

    slot_ids = lax.broadcasted_iota(jnp.int32, (slice_rows, 1), 0)
    causal = lax.broadcasted_iota(jnp.int32, (slice_rows, slice_rows), 0) >= lax.broadcasted_iota(
        jnp.int32, (slice_rows, slice_rows), 1
    )
    triangle = jnp.where(causal, 1.0, 0.0).astype(jnp.float32)
    columns = lax.broadcasted_iota(jnp.int32, (1, width), 1)
    each(n, lambda d: ag_arrival(d).wait_recv())
    low = low_full[...].reshape(slice_rows, width).astype(jnp.float32)

    kept = []
    for j in range(lanes):
        span = pl.ds(j * slice_rows, slice_rows)
        own = (columns >= j * rank) & (columns < (j + 1) * rank)
        gate = acc[span, pl.ds(3 * P_SIZE, P_SIZE)] + dot(jnp.where(own, low, 0.0).astype(jnp.bfloat16), up)
        live = jnp.where(slot_ids < len_ref[j, seq], 1.0, 0.0).astype(jnp.float32)
        step_log = -(live * rate_ref[...] * (2.0 * jax.nn.sigmoid(gate)))
        cumul = dot(triangle, step_log, HIGHEST)
        query = acc[span, pl.ds(0, P_SIZE)].astype(jnp.bfloat16).astype(jnp.float32)
        key = acc[span, pl.ds(P_SIZE, P_SIZE)].astype(jnp.bfloat16).astype(jnp.float32) * (
            live * P_SIZE ** (-0.5)
        )
        value = acc[span, pl.ds(2 * P_SIZE, P_SIZE)].astype(jnp.bfloat16).astype(jnp.float32)
        last = cumul[slice_rows - 1 :, :]
        carried = lax.dot_general(
            key * jnp.exp(last - cumul),
            value,
            (((0,), (0,)), ((), ())),
            precision=HIGHEST,
            preferred_element_type=jnp.float32,
        )
        st_send[j, pl.ds(0, P_SIZE), :] = carried
        st_send[j, pl.ds(P_SIZE, 8), :] = jnp.broadcast_to(jnp.exp(last), (8, P_SIZE))
        kept.append((live, query * jnp.exp(cumul), key * jnp.exp(-cumul), value))

    def st_copy(d):
        return pltpu.make_async_remote_copy(
            src_ref=st_send,
            dst_ref=st_recv.at[seq],
            send_sem=st_ssem.at[d],
            recv_sem=st_rsem.at[d],
            device_id={"seq": lax.rem(seq + d, n_seq)},
            device_id_type=MESH,
        )

    def st_arrival(d):
        peer = lax.rem(seq + n_seq - d, n_seq)
        return pltpu.make_async_remote_copy(
            src_ref=st_send,
            dst_ref=st_recv.at[peer],
            send_sem=st_ssem.at[d],
            recv_sem=st_rsem.at[d],
            device_id={"seq": peer},
            device_id_type=MESH,
        )

    each(n_seq, lambda d: st_copy(d).start())
    st_recv[seq] = st_send[...]

    inners = []
    for j in range(lanes):
        live, query_decay, key_decay, value = kept[j]
        scores = lax.dot_general(
            query_decay,
            key_decay,
            (((1,), (1,)), ((), ())),
            precision=HIGHEST,
            preferred_element_type=jnp.float32,
        )
        inners.append(dot(jnp.where(causal, scores, 0.0), value, HIGHEST))

    each(n_seq, lambda d: st_arrival(d).wait_recv())
    for j in range(lanes):
        live, query_decay, _, _ = kept[j]
        span = pl.ds(j * slice_rows, slice_rows)
        ended = jnp.zeros((P_SIZE, P_SIZE), jnp.float32)
        start = ended
        final = ended
        for k in range(n_seq):
            if k:
                same = jnp.where(span_ref[j, k] == span_ref[j, k - 1], 1.0, 0.0).astype(jnp.float32)
                begun = same * ended
            else:
                begun = ended
            decay = jnp.broadcast_to(st_recv[k, j, pl.ds(P_SIZE, 1), :], (P_SIZE, P_SIZE)).T
            ended = decay * begun + st_recv[k, j, pl.ds(0, P_SIZE), :]
            at = jnp.where(seq == k, 1.0, 0.0).astype(jnp.float32)
            start = start + at * begun
            final = final + at * ended
        inner = inners[j] + dot(query_decay, start, HIGHEST)
        scale = lax.rsqrt(jnp.maximum(jnp.mean(inner * inner, axis=-1, keepdims=True), NORM_FLOOR))
        out_ref[span, :] = (inner * scale * gain_ref[...] * live).astype(jnp.bfloat16)
        state_ref[0, j] = final

    each(n, lambda d: up_copy(d).wait_send())
    each(n, lambda d: rs_copy(d).wait_send())
    each(n, lambda d: ag_copy(d).wait_send())
    each(n_seq, lambda d: st_copy(d).wait_send())
    for p in range(PIECES):
        for direction in range(2):
            hop(direction, 1, p, own=True).wait_send()
    for direction in range(2):
        for p in range(PIECES):
            reach = half if long_way(direction, p) else half - 1

            def drained(step, carry):
                hop(direction, step, p).wait_send()
                return carry

            lax.fori_loop(2, reach + 1, drained, 0)


def halves(a):
    high = a.astype(jnp.bfloat16)
    return high, (a - high.astype(jnp.float32)).astype(jnp.bfloat16)


def across_rows(a, b):
    return lax.dot_general(a, b, (((1,), (1,)), ((), ())), preferred_element_type=jnp.float32)


def down_rows(a, b):
    return lax.dot_general(a, b, (((0,), (0,)), ((), ())), preferred_element_type=jnp.float32)


def paired_kernel(
    span_ref,
    prompt_ref,
    owner_ref,
    len_ref,
    tok_ref,
    w_hbm,
    down_hbm,
    up_ref,
    rate_ref,
    gain_ref,
    out_ref,
    state_ref,
    tokbuf,
    wbuf,
    dturn,
    dsend,
    din,
    dbuf,
    acc,
    lacc,
    lowb,
    upsend,
    upin,
    upsum,
    upr,
    rgbuf,
    qdh,
    qdl,
    inn,
    run,
    carry,
    st_send,
    st_recv,
    obuf,
    fbuf,
    w_sem,
    t_local,
    t_send,
    t_recv,
    f_send,
    wz_send,
    wz_recv,
    wy_send,
    wy_recv,
    wc_send,
    wc_recv,
    r_send,
    r_recv,
    p_send,
    p_recv,
    u_send,
    u_recv,
    l_send,
    l_recv,
    s_send,
    s_recv,
    o_send,
    o_recv,
    e_send,
    e_recv,
    o_local,
):
    h = lax.axis_index("head")
    s = lax.axis_index("seq")
    z, x = lax.div(h, 2), lax.rem(h, 2)
    y, k = lax.div(s, 2), lax.rem(s, 2)
    b, p = lax.div(z, 2), lax.rem(z, 2)
    zi, z2, z3 = z + 1 - 2 * p, lax.rem(z + 2, 4), 3 - z
    same = k == p
    differ = k != p
    inner = (z == 1) | (z == 2)
    outer = (z == 0) | (z == 3)
    inward = 1 + p
    seqc = 2 * y + p
    lane = k

    rows, shard = tok_ref.shape
    lanes = span_ref.shape[0]
    per_owner, rank, model = down_hbm.shape
    slice_rows = rows // lanes
    chunk = slice_rows // CHUNKS
    deep_part = model // W_PARTS
    wide = 4 * P_SIZE

    def at(xx, yy, zz, kk):
        return {"head": 2 * zz + xx, "seq": 2 * yy + kk}

    def remote(src, dst, send, recv, where):
        return pltpu.make_async_remote_copy(
            src_ref=src, dst_ref=dst, send_sem=send, recv_sem=recv, device_id=where, device_id_type=MESH
        )

    loads = [
        pltpu.make_async_copy(
            w_hbm.at[c],
            wbuf.at[:, pl.ds(pl.multiple_of(p * wide + c * P_SIZE, P_SIZE), P_SIZE)],
            w_sem.at[c],
        )
        for c in range(4)
    ]
    pools = pltpu.make_async_copy(down_hbm, dturn, w_sem.at[4])

    barrier = pltpu.get_barrier_semaphore()
    plane = 2 * h + k

    def greet(d, c):
        other = lax.rem(plane + d, 16)
        where = {"head": lax.div(other, 2), "seq": 2 * y + lax.rem(other, 2)}
        pl.semaphore_signal(barrier, inc=1, device_id=where, device_id_type=MESH)
        return c

    lax.fori_loop(1, 16, greet, 0)
    for zz in (z, zi):
        pl.semaphore_signal(barrier, inc=1, device_id=at(x, 1 - y, zz, k), device_id_type=MESH)
    pools.start()
    rgbuf[p, pl.ds(0, 1), :] = rate_ref[...]
    rgbuf[p, pl.ds(1, 1), :] = gain_ref[...]
    st_recv[...] = jnp.zeros_like(st_recv)
    pl.semaphore_wait(barrier, 17)

    def deep_at(i):
        return pl.ds(pl.multiple_of(i * deep_part, 128), deep_part)

    def col_at(q, c):
        return pl.ds(pl.multiple_of(q * wide + c * P_SIZE, P_SIZE), P_SIZE)

    def wz_copy(i):
        c = 2 * y + k
        return remote(
            w_hbm.at[c, deep_at(i)],
            wbuf.at[deep_at(i), col_at(p, c)],
            wz_send.at[i],
            wz_recv.at[i],
            at(x, y, zi, k),
        )

    def held(i, c):
        return wbuf.at[deep_at(i), col_at(1 - p, c)]

    def wz_arrival(i):
        c = 2 * y + k
        return remote(held(i, c), held(i, c), wz_send.at[i], wz_recv.at[i], at(x, y, zi, k))

    def wy_copy(i):
        c = 2 * y + k
        return remote(held(i, c), held(i, c), wy_send.at[i], wy_recv.at[i], at(x, 1 - y, z, k))

    def wy_arrival(i):
        c = 2 * (1 - y) + k
        return remote(held(i, c), held(i, c), wy_send.at[i], wy_recv.at[i], at(x, 1 - y, z, k))

    def wc_copy(g, i):
        c = 2 * (y + g - 2 * y * g) + k
        return remote(held(i, c), held(i, c), wc_send.at[g, i], wc_recv.at[g, i], at(x, y, z, 1 - k))

    def wc_arrival(g, i):
        c = 2 * (y + g - 2 * y * g) + 1 - k
        return remote(held(i, c), held(i, c), wc_send.at[g, i], wc_recv.at[g, i], at(x, y, z, 1 - k))

    def each(first, count, act):
        def turn(i, c):
            act(i)
            return c

        lax.fori_loop(first, count, turn, 0)

    each(0, 2, lambda i: wz_copy(i).start())

    def mask(seq):
        spot = owner_ref[prompt_ref[span_ref[lane, seq]]]
        return [jnp.where(spot == h * per_owner + i, 1.0, 0.0).astype(jnp.float32) for i in range(per_owner)]

    mine, theirs = mask(seqc), mask(2 * y + 1 - p)
    for g in range(4):
        for q in range(2):
            head = 4 * (g // 2) + 2 * q + g % 2
            part = [up_ref[o, :, head * P_SIZE : (head + 1) * P_SIZE].astype(jnp.float32) for o in range(per_owner)]
            upsend[g, q] = sum(theirs[o] * part[o] for o in range(per_owner)).astype(jnp.bfloat16)
            upsum[g, q] = sum(mine[o] * part[o] for o in range(per_owner)).astype(jnp.bfloat16)

    from_outer = jnp.where(inner, 1, 0)
    pan_copy = remote(dsend, din.at[from_outer], p_send.at[0], p_recv.at[from_outer], at(x, y, inward, k))
    upp_copy = remote(upsend, upin.at[from_outer], p_send.at[1], p_recv.at[2 + from_outer], at(x, y, inward, k))
    upp_copy.start()
    each(2, W_PARTS, lambda i: wz_copy(i).start())
    for load in loads:
        load.start()

    rg_copy = remote(rgbuf.at[p], rgbuf.at[p], r_send, r_recv, at(x, y, zi, k))
    rg_arrival = remote(rgbuf.at[1 - p], rgbuf.at[1 - p], r_send, r_recv, at(x, y, zi, k))
    rg_copy.start()

    def chunk_at(r):
        return pl.ds(pl.multiple_of(r * chunk, chunk), chunk)

    def place(f, r):
        return tokbuf.at[chunk_at(r), pl.ds(pl.multiple_of(f * shard, 128), shard)]

    def tok_copy(t, j, r, where):
        source = tok_ref.at[pl.ds(pl.multiple_of(j * slice_rows + r * chunk, chunk), chunk)]
        return remote(source, place(h, r), t_send.at[t, j, r], t_recv.at[h, r], where)

    def free_sends(r, act):
        @pl.when(same)
        def _():
            act(tok_copy(0, 1 - k, r, at(x, y, z, 1 - k)))
            for j in range(2):
                act(tok_copy(1, j, r, at(1 - x, y, z, j)))

        @pl.when(differ & inner)
        def _():
            for j in range(2):
                act(tok_copy(2, j, r, at(x, y, z3, j)))

    def late_sends(r, act):
        @pl.when(same)
        def _():
            for j in range(2):
                act(tok_copy(2, j, r, at(x, y, z2, j)))

        @pl.when(differ)
        def _():
            for j in range(2):
                act(tok_copy(1, j, r, at(x, y, zi, j)))

    own = pltpu.make_async_copy(
        tok_ref.at[pl.ds(pl.multiple_of(lane * slice_rows, chunk), slice_rows)],
        tokbuf.at[:, pl.ds(pl.multiple_of(h * shard, 128), shard)],
        t_local,
    )

    each(0, CHUNKS, lambda r: free_sends(r, lambda copy: copy.start()))

    @pl.when(same)
    def _():
        own.start()

    pools.wait()
    half_model = model // 2
    strips = 6
    strip = half_model // strips

    def strip_at(i, base=0):
        return pl.ds(pl.multiple_of(base + i * strip, 128), strip)

    def pick(weights, i):
        both = [
            sum(weights[o] * dturn[o, :, strip_at(i, base)].astype(jnp.float32) for o in range(per_owner))
            for base in (0, half_model)
        ]
        return jnp.concatenate(both, axis=0).astype(jnp.bfloat16).T

    def fill(i):
        dsend[strip_at(i), :] = pick(theirs, i)
        dbuf[strip_at(i), :] = pick(mine, i)

    each(0, strips, fill)

    def arrived(f, r):
        remote(place(f, r), place(f, r), t_send.at[0, 0, 0], t_recv.at[f, r], at(1 - x, y, z, k)).wait_recv()

    def x_forward(a, zz, r):
        f = 2 * zz + x
        return remote(place(f, r), place(f, r), f_send.at[a - 1, r], t_recv.at[f, r], at(1 - x, y, z, k))

    def z_forward(r):
        f = 2 * zi + x
        return remote(place(f, r), place(f, r), f_send.at[3, r], t_recv.at[f, r], at(x, y, z2, k))

    @pl.when(inner)
    def _():
        pan_copy.start()

    mates = [None, at(1 - x, y, z, k), at(x, y, z2, k), at(1 - x, y, z2, k)]
    groups = [2 * b + x, 2 * b + 1 - x, 2 * (1 - b) + x, 2 * (1 - b) + 1 - x]

    def up_copy(d):
        return remote(upsum.at[groups[d]], upr.at[d], u_send.at[d], u_recv.at[d], mates[d])

    @pl.when(outer)
    def _():
        for d in range(1, 4):
            up_copy(d).start()

    def spread(i, c):
        wz_arrival(i).wait_recv()
        wy_copy(i).start()
        wc_copy(0, i).start()

        @pl.when(i > 0)
        def _():
            wy_arrival(i - 1).wait_recv()
            wc_copy(1, i - 1).start()

        @pl.when(inner & (lax.rem(i, W_PARTS // CHUNKS) == 0))
        def _():
            r = lax.div(i, W_PARTS // CHUNKS)
            arrived(2 * z3 + x, r)
            x_forward(3, z3, r).start()

        @pl.when(inner & (i == 4))
        def _():
            whole = upsum[...].astype(jnp.float32)
            for g in range(2):
                remote(upsend, upin.at[g], p_send.at[1], p_recv.at[2 + g], at(x, y, zi, k)).wait_recv()
                whole = whole + upin[g].astype(jnp.float32)
            upsum[...] = whole.astype(jnp.bfloat16)
            for d in range(1, 4):
                up_copy(d).start()

        @pl.when((i == LATE) & outer)
        def _():
            pan_copy.start()

        @pl.when(i == LATE)
        def _():
            each(0, CHUNKS, lambda r: late_sends(r, lambda copy: copy.start()))

        @pl.when(outer & (i >= W_PARTS - CHUNKS))
        def _():
            r = i - (W_PARTS - CHUNKS)
            arrived(2 * z2 + x, r)
            x_forward(2, z2, r).start()

        return c

    lax.fori_loop(0, W_PARTS, spread, 0)
    wy_arrival(W_PARTS - 1).wait_recv()
    wc_copy(1, W_PARTS - 1).start()

    def gather_down():
        @pl.when(inner)
        def _():
            for g in range(2):
                remote(dsend, din.at[g], p_send.at[0], p_recv.at[g], at(x, y, zi, k)).wait_recv()

            def turn(i):
                whole = dbuf[strip_at(i), :].astype(jnp.float32)
                for g in range(2):
                    whole = whole + din[g, strip_at(i), :].astype(jnp.float32)
                dbuf[strip_at(i), :] = whole.astype(jnp.bfloat16)

            each(0, strips, turn)

    upr[0] = upsum[groups[0]]

    def packed_at(r):
        return pl.ds(pl.multiple_of(r * (chunk // 2), chunk // 2), chunk // 2)

    def low_copy(d, r):
        span = packed_at(r)
        return remote(lowb.at[0, span], lowb.at[d, span], l_send.at[d, r], l_recv.at[d, r], mates[d])

    run[...] = jnp.zeros_like(run)
    carry[...] = jnp.zeros_like(carry)

    def shard_of(a, column):
        high, bit = lax.div(a, 2), lax.rem(a, 2)
        zz = 2 * (b + high - 2 * b * high) + p + bit - 2 * p * bit
        return 2 * zz + column

    low_half = lax.div(lax.broadcasted_iota(jnp.int32, (1, P_SIZE), 1), rank)

    def multiply(f, r, first):
        span = chunk_at(r)
        deep = pl.ds(pl.multiple_of(f * shard, 128), shard)
        block = tokbuf[span, deep]
        late = lax.div(f, 4)
        packed = pl.ds(pl.multiple_of((f - 4 * late) * shard, 128), shard)
        low_part = jnp.where(low_half == late, dot(block, dbuf[packed, :]), 0.0)
        part = dot(block, wbuf[deep, :])

        @pl.when(first)
        def _():
            lacc[...] = low_part
            acc[span, :] = part

        @pl.when(jnp.logical_not(first))
        def _():
            lacc[...] += low_part
            acc[span, :] += part

    def onward(a, zz, r):
        arrived(2 * zz + x, r)
        x_forward(a, zz, r).start()

    def advance(r):
        @pl.when(inner)
        def _():
            onward(1, zi, r)
            z_forward(r).start()
            onward(2, z2, r)

        @pl.when(outer)
        def _():
            onward(3, z3, r)

            @pl.when(r + 2 < CHUNKS)
            def _():
                onward(1, zi, r + 2)

        @pl.when(differ)
        def _():
            arrived(h, r)

        @pl.when(same & (r == 0))
        def _():
            own.wait()

    soon = jnp.where(inner, 3, 2)

    def other(a, r):
        f = shard_of(a, 1 - x)
        arrived(f, r)
        multiply(f, r, a < 0)

    def early(r):
        each(0, 4, lambda a: multiply(shard_of(a, x), r, a == 0))
        each(0, 2, lambda i: other(i * soon, r))

    def finish(r):
        second, step_to = jnp.where(inner, 2, 1), jnp.where(inner, -1, 2)
        each(0, 2, lambda i: other(second + i * step_to, r))
        low_sum = (lacc[:, :rank] + lacc[:, rank:]).astype(jnp.bfloat16)
        lowb[0, packed_at(r), :] = jnp.concatenate([low_sum[: chunk // 2], low_sum[chunk // 2 :]], axis=1)
        for d in (3, 2, 1):
            low_copy(d, r).start()

    row_ids = lax.broadcasted_iota(jnp.int32, (chunk, chunk), 0)
    column_ids = lax.broadcasted_iota(jnp.int32, (chunk, chunk), 1)
    causal = row_ids >= column_ids
    triangle = jnp.where(causal, 1.0, 0.0).astype(jnp.bfloat16)
    slot_ids = lax.broadcasted_iota(jnp.int32, (slice_rows, 1), 0)
    chunk_ids = lax.broadcasted_iota(jnp.int32, (chunk, 1), 0)
    length = len_ref[lane, seqc]

    def state_copy(d):
        where = [None, at(x, 1 - y, z, k), at(x, y, zi, k), at(x, 1 - y, zi, k)][d]
        return remote(st_send, st_recv.at[seqc], s_send.at[d], s_recv.at[d], where)

    def later(d, act, side=0):
        pl.when((p if d == 2 else y) == side)(lambda: act())

    def state_arrival(d):
        yy, pp = [None, (1 - y, p), (y, 1 - p), (1 - y, 1 - p)][d]
        return remote(st_send, st_recv.at[2 * yy + pp], s_send.at[d], s_recv.at[d], at(x, 1 - y, z, k))

    def attend(r):
        span = chunk_at(r)

        @pl.when(r == 0)
        def _():
            for d in range(1, 4):
                up_copy(d).wait_recv()
            for q in range(2):
                upr[0, q] = sum(upr[d, q].astype(jnp.float32) for d in range(4)).astype(jnp.bfloat16)

        for d in range(1, 4):
            low_copy(d, r).wait_recv()
        low = sum(lowb[d, packed_at(r), :].astype(jnp.float32) for d in range(4)).astype(jnp.bfloat16)
        low = jnp.concatenate([low[:, :rank], low[:, rank:]], axis=0)
        live = jnp.where(chunk_ids + r * chunk < length, 1.0, 0.0).astype(jnp.float32)
        kept = []
        for q in range(2):
            first = q * wide
            gate = acc[span, first + 3 * P_SIZE : first + 4 * P_SIZE] + dot(low, upr[0, q])
            step_log = -(live * rgbuf[q, pl.ds(0, 1), :] * (2.0 * jax.nn.sigmoid(gate)))
            a0, rest = halves(step_log)[0], step_log
            rest = rest - a0.astype(jnp.float32)
            a1, a2 = halves(rest)
            cumul = dot(triangle, a0) + (dot(triangle, a1) + dot(triangle, a2)) + carry[q, pl.ds(0, 1), :]
            carry[q] = jnp.broadcast_to(cumul[chunk - 1 :, :], (8, P_SIZE))
            query = acc[span, first : first + P_SIZE].astype(jnp.bfloat16).astype(jnp.float32)
            key = acc[span, first + P_SIZE : first + 2 * P_SIZE].astype(jnp.bfloat16).astype(jnp.float32) * (
                live * P_SIZE ** (-0.5)
            )
            value = acc[span, first + 2 * P_SIZE : first + 3 * P_SIZE].astype(jnp.bfloat16)
            q_high, q_low = halves(query * jnp.exp(cumul))
            k_high, k_low = halves(key * jnp.exp(-cumul))
            qdh[q, span, :] = q_high
            qdl[q, span, :] = q_low
            before = run[q]
            run[q] = before + (down_rows(k_high, value) + down_rows(k_low, value))
            kept.append((q_high, q_low, k_high, k_low, value, before))

        @pl.when(r == CHUNKS - 1)
        def _():
            for q in range(2):
                st_send[q, pl.ds(0, P_SIZE), :] = run[q]
                st_send[q, pl.ds(P_SIZE, 8), :] = jnp.exp(carry[q])
            for d in (3, 1, 2):
                later(d, state_copy(d).start)
            st_recv[seqc] = st_send[...]

        for q in range(2):
            q_high, q_low, k_high, k_low, value, before = kept[q]
            scores = across_rows(q_high, k_high) + (across_rows(q_high, k_low) + across_rows(q_low, k_high))
            s_high, s_low = halves(jnp.where(causal, scores, 0.0))
            b_high, b_low = halves(before)
            inn[q, span, :] = (
                dot(s_high, value)
                + dot(s_low, value)
                + dot(q_high, b_high)
                + (dot(q_high, b_low) + dot(q_low, b_high))
            )

    @pl.when(outer)
    def _():
        each(0, 2, lambda r: onward(1, zi, r))

    for i in range(4):
        loads[i].wait()
    each(0, W_PARTS, lambda i: wc_arrival(0, i).wait_recv())
    each(0, W_PARTS, lambda i: wc_arrival(1, i).wait_recv())
    rg_arrival.wait_recv()
    def step(t, c):
        @pl.when(t < CHUNKS)
        def _():
            advance(t)

        @pl.when(t == 0)
        def _():
            gather_down()

        @pl.when((t > 0) & (t <= CHUNKS))
        def _():
            finish(t - 1)

        @pl.when(t < CHUNKS)
        def _():
            early(t)

        @pl.when(t > 2)
        def _():
            attend(t - 3)

        return c

    lax.fori_loop(0, CHUNKS + 3, step, 0)

    for d in range(1, 4):
        later(d, state_arrival(d).wait_recv, 1)
    alive = jnp.where(slot_ids < length, 1.0, 0.0).astype(jnp.float32)

    def out_copy(q, where):
        return remote(
            obuf.at[q],
            out_ref.at[pl.ds(pl.multiple_of(lane * slice_rows, chunk), slice_rows)],
            o_send.at[q],
            o_recv.at[lane],
            where,
        )

    def end_copy(q, where):
        return remote(fbuf.at[q], state_ref.at[0, lane], e_send.at[q], e_recv.at[lane], where)

    keep_out = pltpu.make_async_copy(
        obuf.at[p], out_ref.at[pl.ds(pl.multiple_of(lane * slice_rows, chunk), slice_rows)], o_local.at[0]
    )
    keep_end = pltpu.make_async_copy(fbuf.at[p], state_ref.at[0, lane], o_local.at[1])
    away, beside = at(x, y, zi, p), at(x, y, z, 1 - k)

    for i in range(2):
        q = 1 - p if i == 0 else p
        ended = jnp.zeros((P_SIZE, P_SIZE), jnp.float32)
        start = ended
        final = ended
        for g in range(4):
            if g:
                kin = jnp.where(span_ref[lane, g] == span_ref[lane, g - 1], 1.0, 0.0).astype(jnp.float32)
                begun = kin * ended
            else:
                begun = ended
            decay = jnp.broadcast_to(st_recv[g, q, pl.ds(P_SIZE, 1), :], (P_SIZE, P_SIZE)).T
            ended = decay * (begun + st_recv[g, q, pl.ds(0, P_SIZE), :])
            now = jnp.where(seqc == g, 1.0, 0.0).astype(jnp.float32)
            start = start + now * begun
            final = final + now * ended
        fbuf[q] = final
        b_high, b_low = halves(start)
        total = inn[q] + dot(qdh[q], b_high) + (dot(qdh[q], b_low) + dot(qdl[q], b_high))
        scale = lax.rsqrt(jnp.maximum(jnp.mean(total * total, axis=-1, keepdims=True), NORM_FLOOR))
        obuf[q] = (total * scale * rgbuf[q, pl.ds(1, 1), :] * alive).astype(jnp.bfloat16)
        if i == 0:
            end_copy(q, away).start()
            out_copy(q, away).start()
        else:

            @pl.when(same)
            def _():
                keep_end.start()
                keep_out.start()

            @pl.when(differ)
            def _():
                end_copy(p, beside).start()
                out_copy(p, beside).start()

    def landed(j):
        span = pl.ds(pl.multiple_of(j * slice_rows, chunk), slice_rows)
        remote(obuf.at[0], out_ref.at[span], o_send.at[0], o_recv.at[j], beside).wait_recv()
        remote(fbuf.at[0], state_ref.at[0, j], e_send.at[0], e_recv.at[j], beside).wait_recv()

    landed(1 - k)

    @pl.when(same)
    def _():
        keep_end.wait()
        keep_out.wait()

    @pl.when(differ)
    def _():
        landed(k)
        end_copy(p, beside).wait_send()
        out_copy(p, beside).wait_send()

    end_copy(1 - p, away).wait_send()
    out_copy(1 - p, away).wait_send()
    each(0, W_PARTS, lambda i: wz_copy(i).wait_send())
    each(0, W_PARTS, lambda i: wy_copy(i).wait_send())
    each(0, W_PARTS, lambda i: wc_copy(0, i).wait_send())
    each(0, W_PARTS, lambda i: wc_copy(1, i).wait_send())
    rg_copy.wait_send()
    pan_copy.wait_send()
    upp_copy.wait_send()
    for d in range(1, 4):
        up_copy(d).wait_send()
        later(d, state_copy(d).wait_send)

    def drained(r):
        free_sends(r, lambda copy: copy.wait_send())
        late_sends(r, lambda copy: copy.wait_send())
        for a, zz in ((1, zi), (2, z2), (3, z3)):
            x_forward(a, zz, r).wait_send()

        @pl.when(inner)
        def _():
            z_forward(r).wait_send()

        for d in range(1, 4):
            low_copy(d, r).wait_send()

    each(0, CHUNKS, drained)


def paired_call(args):
    tokens, proj_weight, decay_rate, norm_gain, pool_down, pool_up, span_id, prompt_adapter, owner_pos, slice_len = args
    rows, shard = tokens.shape
    model = proj_weight.shape[1]
    lanes = span_id.shape[1]
    per_owner, _, rank = pool_down.shape
    slice_rows = rows // lanes
    smem = pl.BlockSpec(memory_space=pltpu.SMEM)
    vmem = pl.BlockSpec(memory_space=pltpu.VMEM)
    hbm = pl.BlockSpec(memory_space=pl.ANY)
    dma = pltpu.SemaphoreType.DMA
    bf16, f32 = jnp.bfloat16, jnp.float32
    chunk = slice_rows // CHUNKS
    return pl.pallas_call(
        paired_kernel,
        out_shape=(
            jax.ShapeDtypeStruct((rows, P_SIZE), bf16),
            jax.ShapeDtypeStruct((1, lanes, P_SIZE, P_SIZE), f32),
        ),
        in_specs=[smem, smem, smem, smem, vmem, hbm, hbm, vmem, vmem, vmem],
        out_specs=(vmem, vmem),
        scratch_shapes=[
            pltpu.VMEM((slice_rows, model), bf16),
            pltpu.VMEM((model, 8 * P_SIZE), bf16),
            pltpu.VMEM((per_owner, rank, model), bf16),
            pltpu.VMEM((model // 2, P_SIZE), bf16),
            pltpu.VMEM((2, model // 2, P_SIZE), bf16),
            pltpu.VMEM((model // 2, P_SIZE), bf16),
            pltpu.VMEM((slice_rows, 8 * P_SIZE), f32),
            pltpu.VMEM((chunk, P_SIZE), f32),
            pltpu.VMEM((4, slice_rows // 2, P_SIZE), bf16),
            pltpu.VMEM((4, 2, rank, P_SIZE), bf16),
            pltpu.VMEM((2, 4, 2, rank, P_SIZE), bf16),
            pltpu.VMEM((4, 2, rank, P_SIZE), bf16),
            pltpu.VMEM((4, 2, rank, P_SIZE), bf16),
            pltpu.VMEM((2, 8, P_SIZE), f32),
            pltpu.VMEM((2, slice_rows, P_SIZE), bf16),
            pltpu.VMEM((2, slice_rows, P_SIZE), bf16),
            pltpu.VMEM((2, slice_rows, P_SIZE), f32),
            pltpu.VMEM((2, P_SIZE, P_SIZE), f32),
            pltpu.VMEM((2, 8, P_SIZE), f32),
            pltpu.VMEM((2, P_SIZE + 8, P_SIZE), f32),
            pltpu.VMEM((4, 2, P_SIZE + 8, P_SIZE), f32),
            pltpu.VMEM((2, slice_rows, P_SIZE), bf16),
            pltpu.VMEM((2, P_SIZE, P_SIZE), f32),
            dma((5,)),
            dma,
            dma((3, 2, CHUNKS)),
            dma((8, CHUNKS)),
            dma((4, CHUNKS)),
            dma((W_PARTS,)),
            dma((W_PARTS,)),
            dma((W_PARTS,)),
            dma((W_PARTS,)),
            dma((2, W_PARTS)),
            dma((2, W_PARTS)),
            dma,
            dma,
            dma((2,)),
            dma((4,)),
            dma((4,)),
            dma((4,)),
            dma((4, CHUNKS)),
            dma((4, CHUNKS)),
            dma((4,)),
            dma((4,)),
            dma((2,)),
            dma((2,)),
            dma((2,)),
            dma((2,)),
            dma((2,)),
        ],
        compiler_params=pltpu.CompilerParams(
            collective_id=0, has_side_effects=True, vmem_limit_bytes=58 * 1024 * 1024
        ),
    )(
        span_id.T,
        prompt_adapter,
        owner_pos,
        slice_len.T,
        tokens,
        proj_weight,
        jnp.swapaxes(pool_down, 1, 2),
        pool_up,
        decay_rate.reshape(1, -1),
        norm_gain.reshape(1, -1),
    )


def solution(mesh):
    n, n_seq = mesh.shape["head"], mesh.shape["seq"]

    def body(
        tokens,
        proj_weight,
        decay_rate,
        norm_gain,
        pool_down,
        pool_up,
        span_id,
        prompt_adapter,
        owner_pos,
        slice_len,
    ):
        if n == 8 and n_seq == 4 and span_id.shape[1] == 2:
            return paired_call(
                (
                    tokens,
                    proj_weight,
                    decay_rate,
                    norm_gain,
                    pool_down,
                    pool_up,
                    span_id,
                    prompt_adapter,
                    owner_pos,
                    slice_len,
                )
            )
        rows, shard = tokens.shape
        model = proj_weight.shape[1]
        lanes = span_id.shape[1]
        per_owner, _, rank = pool_down.shape
        slice_rows = rows // lanes
        width = lanes * rank
        smem = pl.BlockSpec(memory_space=pltpu.SMEM)
        vmem = pl.BlockSpec(memory_space=pltpu.VMEM)
        hbm = pl.BlockSpec(memory_space=pl.ANY)
        dma = pltpu.SemaphoreType.DMA
        return pl.pallas_call(
            functools.partial(ring_kernel, n, n_seq),
            out_shape=(
                jax.ShapeDtypeStruct((rows, P_SIZE), jnp.bfloat16),
                jax.ShapeDtypeStruct((1, lanes, P_SIZE, P_SIZE), jnp.float32),
            ),
            in_specs=[smem, smem, smem, smem, vmem, hbm, hbm, vmem, vmem, vmem],
            out_specs=(vmem, vmem),
            scratch_shapes=[
                pltpu.VMEM((2, n // 2, rows, shard), jnp.bfloat16),
                pltpu.VMEM((model, 4 * P_SIZE), jnp.bfloat16),
                pltpu.VMEM((per_owner, model, rank), jnp.bfloat16),
                pltpu.VMEM((per_owner, rank, model), jnp.bfloat16),
                pltpu.VMEM((rows, 4 * P_SIZE), jnp.float32),
                pltpu.VMEM((per_owner, rows, rank), jnp.float32),
                pltpu.VMEM((n, width, P_SIZE), jnp.bfloat16),
                pltpu.VMEM((n, width, P_SIZE), jnp.bfloat16),
                pltpu.VMEM((slice_rows, width), jnp.bfloat16),
                pltpu.VMEM((n, slice_rows // n, width), jnp.bfloat16),
                pltpu.VMEM((n, slice_rows // n, width), jnp.bfloat16),
                pltpu.VMEM((lanes, P_SIZE + 8, P_SIZE), jnp.float32),
                pltpu.VMEM((n_seq, lanes, P_SIZE + 8, P_SIZE), jnp.float32),
                dma((5,)),
                dma((2, n // 2, PIECES)),
                dma((2, n // 2, PIECES)),
                dma((n,)),
                dma((n,)),
                dma((n,)),
                dma((n,)),
                dma((n,)),
                dma((n,)),
                dma((n_seq,)),
                dma((n_seq,)),
            ],
            compiler_params=pltpu.CompilerParams(
                collective_id=0, has_side_effects=True, vmem_limit_bytes=58 * 1024 * 1024
            ),
        )(
            span_id.T,
            prompt_adapter,
            owner_pos,
            slice_len.T,
            tokens,
            proj_weight,
            jnp.swapaxes(pool_down, 1, 2),
            pool_up,
            decay_rate.reshape(1, -1),
            norm_gain.reshape(1, -1),
        )

    in_specs = (
        P("seq", "head"),
        P(None, None, "head"),
        P("head"),
        P("head"),
        P("head", None, None),
        P("head", None, None),
        P(),
        P(),
        P(),
        P(),
    )
    out_specs = (P("seq", "head"), P("seq", None, "head", None))
    return jax.shard_map(body, mesh=mesh, in_specs=in_specs, out_specs=out_specs, check_vma=False)
```
